32 devices in a mesh: chain: 2 (over y), px: 8 (over z, x), py: 2 (over core).
Axes of the slice: x: 2, y: 2, z: 4, core: 2. Of those that a mesh axis runs over, the one named last changes fastest.
Arguments:
- adjoint: float32 [512, 256, 256], P(('chain', 'px'), 'py'), parts along dimension 0, may hold values from -6 to 6
- saved: float32 [512, 256, 256], P(('chain', 'px'), 'py'), parts along dimension 0, may hold values from -6 to 6
- spectra: bfloat16 [2, 256, 256, 256], P(None, None, 'px'), may hold values from -6 to 6, as said below
- freq_index: int32 [8], replicated, may hold values from 1 to 8
- picked: int32 [2], replicated, may hold values from 0 to 7
Outputs:
- force: float32 [512, 256, 256], P(('chain', 'px'), 'py'), parts along dimension 0
The draws below stay inside these ranges and needn't reach their ends.
There are 2 independent parts, one for each index of `chain`. The reference program is written for one: setup_inputs(seed, part) draws one part's arguments, and reference() takes and returns one part's arrays. A program takes and returns all parts, laid end to end along the dimension named above; an argument that names none is the same for every part. Nothing has to cross between parts.
Inputs may be any that keep to these rules, and one draw needn't show every extreme that they name: Each kernel is even in every momentum coordinate separately: spectra[j][k1, k2, k3] is unchanged when k1 is replaced by (256 - k1) mod 256, and likewise k2 with 256 and k3 with 256.
All inputs are finite; a program needn't handle non-finite values.
Results may differ from the reference program's by a relative error of at most 0.0003.
Values sent between devices are 32-bit elements; how exact they have to be, the bound alone decides.
A program may use at most 128 MiB of HBM per device.

```python
import math
import jax
import jax.numpy as jnp

L1 = 256
L2 = 256
L3 = 256
FEATS = 8
WINDOW = 2


def folded_index(length):
    counter = jnp.arange(length, dtype=jnp.int32)
    return jnp.minimum(counter, length - counter).astype(jnp.int32)


def draw_spectra(key, part):
    reduced = jax.random.normal(key, (WINDOW, L1 // 2 + 1, L2 // 2 + 1, L3 // 2 + 1), jnp.float32)
    reduced = jnp.clip(reduced, -6.0, 6.0)
    expanded = jnp.take(reduced, folded_index(L1), axis=1)
    expanded = jnp.take(expanded, folded_index(L2), axis=2)
    expanded = jnp.take(expanded, folded_index(L3), axis=3)
    return expanded.astype(jnp.bfloat16)


def set_ends(drawn, own_key, low, largest):
    extent = drawn.shape
    index_at = [jax.random.randint(jax.random.fold_in(own_key, axis), (), 0, extent[axis]) for axis in range(len(extent))]
    drawn = drawn.at[tuple(index_at)].set(low)
    longest = extent.index(max(extent))
    index_at[longest] = (index_at[longest] + 1) % extent[longest]
    return drawn.at[tuple(index_at)].set(largest)


def levels(key, shape, shards, smallest, largest):
    factor_of = 1.0
    for position, parts in shards:
        heights = jax.random.uniform(jax.random.fold_in(jax.random.fold_in(key, 6), position), (parts,), jnp.float32, smallest / len(shards), largest / len(shards))
        factor_of = factor_of * jnp.repeat(jnp.exp(heights), shape[position] // parts).reshape((-1,) + (1,) * (len(shape) - 1 - position))
    return factor_of


def scatter_about(rng, dims, scale, reach, shards=(), held_as=jnp.bfloat16):
    gain = levels(rng, dims, shards, -0.22, 0.18) if shards else 1.0
    values = jax.random.normal(rng, dims, jnp.float32) * scale * gain
    return jnp.minimum(jnp.maximum(values, -reach), reach).astype(held_as)


def setup_inputs(seed: int = 0, part: int = 0) -> dict:
    arg_keys = jax.random.split(jax.random.key(seed), 6)
    part_splits = jax.random.split(jax.random.fold_in(arg_keys[5], part), 6)
    return {
        "adjoint": scatter_about(part_splits[0], (L1, L2, L3), 1.0, 6.0, ((0, 8), (1, 2)), jnp.float32),
        "saved": scatter_about(part_splits[1], (L1, L2, L3), 1.0, 6.0, ((0, 8), (1, 2)), jnp.float32),
        "spectra": draw_spectra(jax.random.fold_in(arg_keys[5], 71), part),
        "freq_index": set_ends(jax.random.randint(arg_keys[3], (FEATS,), 1, 9), jax.random.fold_in(arg_keys[3], 1), 1, 8).astype(jnp.int32),
        "picked": jax.random.randint(arg_keys[4], (WINDOW,), 0, FEATS).astype(jnp.int32),
    }


def reference(adjoint, saved, spectra, freq_index, picked):
    spectrum = jnp.fft.fftn(adjoint)
    total = jnp.zeros(adjoint.shape, jnp.float32)
    for slot in range(WINDOW):
        omega = (math.pi / 8.0) * freq_index[picked[slot]].astype(jnp.float32)
        field = jnp.real(jnp.fft.ifftn(spectra[slot].astype(jnp.float32) * spectrum))
        total = total + omega * jnp.cos(omega * saved) * field
    return total
```

```python
import functools
import math

import jax
import jax.numpy as jnp
import numpy as np
from jax import lax
from jax.experimental import pallas as pl
from jax.experimental.pallas import tpu as pltpu
from jax.sharding import PartitionSpec as P


def hartley(length):
    counter = np.arange(length, dtype=np.int64)
    angle = (counter[:, None] * counter[None, :] % length) * (2.0 * np.pi / length)
    return np.cos(angle) + np.sin(angle)


def chosen_index(freq_index, picked):
    ids = jnp.arange(freq_index.shape[0], dtype=jnp.int32)
    return jnp.sum(jnp.where(ids[None, :] == picked[:, None], freq_index[None, :], 0), axis=1)


def along(equation, field, table):
    return jnp.einsum(equation, field, jnp.asarray(table, jnp.float32), precision=lax.Precision.HIGH)


def plain_path(adjoint, saved, spectra, chosen):
    size_px, size_py = lax.axis_size("px"), lax.axis_size("py")
    one, two, three = adjoint.shape[0] * size_px, adjoint.shape[1] * size_py, adjoint.shape[2]
    t_one, t_two, t_three = hartley(one), hartley(two), hartley(three)
    width = three // size_py
    field = along("abc,cz->abz", adjoint, t_three)
    field = lax.all_to_all(field, "py", split_axis=2, concat_axis=1, tiled=True)
    field = along("abc,bz->azc", field, t_two)
    field = lax.all_to_all(field, "px", split_axis=1, concat_axis=0, tiled=True)
    spectrum = along("abc,az->zbc", field, t_one)
    kernels = lax.dynamic_slice_in_dim(spectra, lax.axis_index("py") * width, width, 3)
    omegas = chosen.astype(jnp.float32) * (math.pi / 8.0)
    scale = 1.0 / (one * two * three)
    total = jnp.zeros(saved.shape, jnp.float32)
    for slot in range(chosen.shape[0]):
        back = along("abc,az->zbc", spectrum * kernels[slot].astype(jnp.float32), t_one)
        back = lax.all_to_all(back, "px", split_axis=0, concat_axis=1, tiled=True)
        back = along("abc,bz->azc", back, t_two)
        back = lax.all_to_all(back, "py", split_axis=1, concat_axis=2, tiled=True)
        back = along("abc,cz->abz", back, t_three) * scale
        total = total + omegas[slot] * jnp.cos(omegas[slot] * saved) * back
    return total


def as_three(matrix, axis):
    high = matrix.astype(jnp.bfloat16)
    low = (matrix - high.astype(np.float64)).astype(jnp.bfloat16)
    order = (high, high, low)
    return jnp.asarray(np.concatenate(order, axis=axis))


def split(value, axis):
    high = value.astype(jnp.bfloat16)
    low = (value - high.astype(jnp.float32)).astype(jnp.bfloat16)
    return jnp.concatenate([high, low, high], axis=axis)


def from_right(rows, table):
    return jnp.dot(split(rows, 1), table, preferred_element_type=jnp.float32)


def from_left(table, columns):
    return jnp.dot(table, split(columns, 0), preferred_element_type=jnp.float32)


def params(**more):
    return pltpu.CompilerParams(vmem_limit_bytes=58 << 20, **more)


def core_exchange(step, steps, source, target, sems):
    send_sem, recv_sem, own_sem = sems
    me = lax.axis_index("py")
    other = 1 - me

    def away(at, sender, receiver):
        return pltpu.make_async_remote_copy(
            src_ref=source(receiver, at),
            dst_ref=target(sender, at),
            send_sem=send_sem.at[at],
            recv_sem=recv_sem.at[at],
            device_id={"py": receiver},
            device_id_type=pl.DeviceIdType.MESH,
        )

    def stay(at):
        return pltpu.make_async_copy(source(me, at), target(me, at), own_sem.at[at])

    away(step, me, other).start()
    stay(step).start()

    @pl.when(step == steps - 1)
    def _():
        @pl.loop(0, steps)
        def _(at):
            away(at, me, other).wait_send()
            away(at, other, me).wait_recv()
            stay(at).wait()


def greet_core():
    barrier = pltpu.get_barrier_semaphore()
    other = 1 - lax.axis_index("py")
    pl.semaphore_signal(
        barrier, inc=1, device_id={"py": other}, device_id_type=pl.DeviceIdType.MESH
    )
    pl.semaphore_wait(barrier, 1)


def third_kernel(steps, field_ref, table_ref, out_ref, mine, *sems):
    planes, lines, three = field_ref.shape
    parts, width = mine.shape[0], mine.shape[3]
    step = pl.program_id(0)
    pl.when(step == 0)(greet_core)

    def rows(at):
        return pl.ds(pl.multiple_of(at * planes, planes), planes)

    result = from_right(field_ref[...].reshape(planes * lines, three), table_ref[...])
    for part in range(parts):
        piece = result[:, part * width : (part + 1) * width]
        mine[part, rows(step)] = piece.reshape(planes, lines, width)
    core_exchange(
        step,
        steps,
        lambda part, at: mine.at[part, rows(at)],
        lambda part, at: out_ref.at[part, rows(at)],
        sems,
    )


def second_kernel(field_ref, table_ref, out_ref, held):
    parts, planes, _, width = field_ref.shape
    size_px, local, _, _ = out_ref.shape
    for plane in range(0, planes, 2):
        sides = [
            jnp.concatenate([field_ref[part, at] for part in range(parts)], axis=0)
            for at in (plane, plane + 1)
        ]
        result = from_left(table_ref[...], jnp.concatenate(sides, axis=1))
        held[plane] = result[:, :width]
        held[plane + 1] = result[:, width:]
    for peer in range(size_px):
        out_ref[peer] = jnp.swapaxes(held[:, peer * local : (peer + 1) * local, :], 0, 1)


def second_back_kernel(steps, field_ref, table_ref, out_ref, held, mine, *sems):
    _, groups, local, planes, width = field_ref.shape
    parts, lines = mine.shape[0], mine.shape[3]
    inner = steps // mine.shape[1]
    step = pl.program_id(0) * inner + pl.program_id(1)
    slot = pl.program_id(0)
    begin = pl.program_id(1) * planes
    pl.when(step == 0)(greet_core)
    for group in range(groups):
        held[:, group * local : (group + 1) * local, :] = jnp.swapaxes(field_ref[0, group], 0, 1)
    for plane in range(0, planes, 2):
        columns = jnp.concatenate([held[plane], held[plane + 1]], axis=1)
        result = from_left(table_ref[...], columns)
        for part in range(parts):
            rows = result[part * lines : (part + 1) * lines]
            mine[part, slot, begin + plane] = rows[:, :width]
            mine[part, slot, begin + plane + 1] = rows[:, width:]

    def block(ref):
        return lambda part, at: ref.at[part, at // inner, pl.ds((at % inner) * planes, planes)]

    core_exchange(step, steps, block(mine), block(out_ref), sems)


def cosine_turns(turns):
    turns = turns - jnp.floor(turns + 0.5)
    square = turns * turns * (4.0 * math.pi * math.pi)
    value = jnp.full_like(square, 1.0 / math.factorial(20))
    for order in range(9, -1, -1):
        value = value * square + (-1.0) ** order / math.factorial(2 * order)
    return value


def third_back_kernel(scale, chosen_ref, field_ref, saved_ref, table_ref, out_ref):
    parts, slots, planes, lines, width = field_ref.shape
    three = parts * width
    total = None
    site = saved_ref[...].reshape(planes * lines, three)
    for slot in range(slots):
        sides = [field_ref[part, slot].reshape(planes * lines, width) for part in range(parts)]
        field = from_right(jnp.concatenate(sides, axis=1), table_ref[...])
        index = chosen_ref[slot].astype(jnp.float32)
        weight = cosine_turns(site * (index * (1.0 / 16.0))) * (index * (math.pi / 8.0 * scale))
        total = weight * field if total is None else total + weight * field
    out_ref[...] = total.reshape(planes, lines, three)


def middle_kernel(
    chunks,
    field_ref,
    spectra_ref,
    ahead_ref,
    behind_ref,
    out_ref,
    gathered,
    raw,
    kernels,
    product,
    mate_send,
    next_send,
    go_recv,
    kernel_send,
    kernel_recv,
    kernel_pass,
    extra_send,
    back_send,
    back_recv,
    home_sem,
    own_sem,
    raw_sem,
):
    _, rows_all, planes, width = field_ref.shape
    size_px, slots = gathered.shape[0], raw.shape[0]
    half, count = size_px // 2, rows_all // 2
    held_rows, local = raw.shape[1], raw.shape[2]
    one, middle, quarter = size_px * planes, size_px * planes // 2, local // 2
    two = size_px * local
    step = count // chunks
    lead, depth, early = min(8, chunks), min(3, chunks), min(8, chunks)
    me = lax.axis_index("px")
    part = lax.axis_index("py")
    turn_of = lax.axis_index("chain")
    lower = me < half
    base = jnp.where(lower, 0, half)
    column = lax.rem(me, 2)
    mate = me + 1 - 2 * column
    onward = jnp.where(lower, me + 2, me - 2)
    behind = jnp.where(lower, me - 2, me + 2)
    behind_mate = behind + 1 - 2 * column
    inner = (me >= half - 2) & (me < half + 2)
    outer = jnp.logical_not(inner)
    centre = jnp.where(lower, half - 2, half)

    def to(index):
        return dict(device_id={"px": index}, device_id_type=pl.DeviceIdType.MESH)

    def across():
        return dict(device_id={"chain": 1 - turn_of}, device_id_type=pl.DeviceIdType.MESH)

    def rows(chunk):
        return pl.ds(pl.multiple_of(chunk * 2 * step, 2 * step), 2 * step)

    def to_mate(chunk):
        return pltpu.make_async_remote_copy(
            src_ref=field_ref.at[1 - column, rows(chunk)],
            dst_ref=gathered.at[me, rows(chunk)],
            send_sem=mate_send.at[chunk],
            recv_sem=go_recv.at[me, chunk],
            **to(mate),
        )

    def own_on(chunk):
        return pltpu.make_async_remote_copy(
            src_ref=field_ref.at[column, rows(chunk)],
            dst_ref=gathered.at[me, rows(chunk)],
            send_sem=next_send.at[0, chunk],
            recv_sem=go_recv.at[me, chunk],
            **to(onward),
        )

    def pass_on(kind, owner, chunk):
        return pltpu.make_async_remote_copy(
            src_ref=gathered.at[owner, rows(chunk)],
            dst_ref=gathered.at[owner, rows(chunk)],
            send_sem=next_send.at[kind, chunk],
            recv_sem=go_recv.at[owner, chunk],
            **to(onward),
        )

    def back(slot, chunk, receiver):
        return pltpu.make_async_remote_copy(
            src_ref=product.at[slot, receiver - base, rows(chunk)],
            dst_ref=out_ref.at[slot, column, rows(chunk)],
            send_sem=back_send.at[slot, chunk, receiver - base],
            recv_sem=back_recv.at[slot, chunk, column],
            **to(receiver),
        )

    def back_arrival(slot, chunk, side):
        return pltpu.make_async_remote_copy(
            src_ref=product.at[slot, 0, rows(chunk)],
            dst_ref=out_ref.at[slot, side, rows(chunk)],
            send_sem=back_send.at[slot, chunk, 0],
            recv_sem=back_recv.at[slot, chunk, side],
            **to(mate),
        )

    def home(slot, chunk):
        return pltpu.make_async_copy(
            product.at[slot, me - base, rows(chunk)],
            out_ref.at[slot, column, rows(chunk)],
            home_sem.at[slot, chunk],
        )

    def frequency(place):
        group, at = lax.div(place, count // 2), lax.rem(place, count // 2)
        block = 2 - 2 * group + lax.rem(at, 2)
        return local * block + quarter - 1 - lax.div(at, 2) + quarter * column

    def source(place):
        value = jnp.where(place == count, two // 2, frequency(place))
        above = jnp.where(value == 0, 0, lax.div(two - value, local))
        holder = jnp.where(lower, lax.div(value, local), above)
        row = jnp.where(lower | (value == 0), lax.rem(value, local), lax.rem(two - value, local))
        return jnp.where(place == count, half, holder), row

    def held_at(place):
        holder, row = source(place)
        return jnp.where(holder == me, count + 1 + row, place)

    def firsthand(place):
        return lax.rem(lax.div(place, 2), 2) == turn_of

    def kernel_row(turn):
        offset = quarter - 1 - lax.div(turn, 2) + quarter * lax.rem(turn, 2)
        row = jnp.where(lower, offset, lax.rem(local - offset, local))
        value = jnp.where(lower, local * me + row, two - local * me - row)
        block, inside = lax.div(value, local), lax.rem(value, local)
        side, level = lax.div(inside, quarter), lax.rem(inside, quarter)
        place = jnp.where(block >= 2, 0, count // 2) + 2 * (quarter - 1 - level) + lax.rem(block, 2)
        return row, side, jnp.where(value == two // 2, count, place)

    def kernel_copy(row, place, receiver, sem):
        return pltpu.make_async_remote_copy(
            src_ref=kernels.at[count + 1 + row],
            dst_ref=kernels.at[place],
            send_sem=sem,
            recv_sem=kernel_recv.at[place],
            **to(receiver),
        )

    def each_kernel_row(turn, act):
        row, side, place = kernel_row(turn)

        @pl.when((centre + side != me) & firsthand(place))
        def _():
            act(kernel_copy(row, place, centre + side, kernel_send.at[row]))

    def extra_copy(act):
        for sender, place, receiver in ((0, count - 2, half), (half, count, half - 2)):

            @pl.when((me == sender) & firsthand(jnp.int32(place)))
            def _():
                act(kernel_copy(0, place, jnp.int32(receiver), extra_send))

    def kernel_arrival(place):
        return kernel_copy(0, place, mate, extra_send)

    def kernel_on(place):
        return pltpu.make_async_remote_copy(
            src_ref=kernels.at[place],
            dst_ref=kernels.at[place],
            send_sem=kernel_pass.at[place],
            recv_sem=kernel_recv.at[place],
            **across(),
        )

    def arrives(place):
        return source(place)[0] != me

    leading_place = count - 2

    def pass_kernel(place):
        @pl.when(arrives(place) & firsthand(place))
        def _():
            kernel_arrival(place).wait_recv()
            kernel_on(place).start()

    def await_kernel(place):
        @pl.when(arrives(place) & jnp.logical_not(firsthand(place)))
        def _():
            kernel_arrival(place).wait_recv()

    def with_last(chunk, act):
        @pl.when((chunk == leading_place // step) & (column == 0))
        def _():
            act(jnp.int32(count))

    own = pltpu.make_async_copy(field_ref.at[column], gathered.at[me], own_sem)
    fetch = pltpu.make_async_copy(
        spectra_ref.at[:, pl.ds(0, held_rows), :, pl.ds(part * width, width)], raw, raw_sem
    )
    fetch.start()

    @pl.when(inner)
    def _():
        own.start()

    barrier = pltpu.get_barrier_semaphore()
    everyone = 2 * size_px

    @pl.loop(1, everyone)
    def _(turn):
        peer = lax.rem(turn_of * size_px + me + turn, everyone)
        pl.semaphore_signal(
            barrier,
            inc=1,
            device_id={"chain": lax.div(peer, size_px), "px": lax.rem(peer, size_px)},
            device_id_type=pl.DeviceIdType.MESH,
        )

    pl.semaphore_wait(barrier, everyone - 1)

    def send_own(chunk):
        own_on(chunk).start()
        to_mate(chunk).start()

    def convert():
        fetch.wait()
        block = 16
        for slot in range(slots):

            @pl.loop(0, middle // block)
            def _(at):
                span = pl.ds(pl.multiple_of(at * block, block), block)
                piece = raw[slot, span].astype(jnp.float32)
                kernels[count + 1 :, slot, span, :] = jnp.swapaxes(piece, 0, 1)

            piece = raw[slot, middle : middle + block].astype(jnp.float32)
            kernels[count + 1 :, slot, middle : middle + 8, :] = jnp.swapaxes(piece[:8], 0, 1)

    def relay(chunk):
        pass_on(1, mate, chunk).wait_recv()
        pass_on(1, mate, chunk).start()

        @pl.when(inner)
        def _():
            for kind, owner in ((2, behind), (3, behind_mate)):
                pass_on(kind, owner, chunk).wait_recv()
                pass_on(kind, owner, chunk).start()

        @pl.when(chunk + lead < chunks)
        def _():
            send_own(chunk + lead)

    def relay_kernels(chunk):
        @pl.loop(0, step)
        def _(at):
            pass_kernel(chunk * step + at)

        with_last(chunk, pass_kernel)

    def compute(chunk):
        for owner in (onward, onward + 1 - 2 * column):
            pass_on(1, owner, chunk).wait_recv()
        further = jnp.where(lower, onward + 2, onward - 2)
        for owner in (further, further + 1 - 2 * column):
            pass_on(1, owner, chunk).wait_recv()

        @pl.loop(0, step)
        def _(at):
            await_kernel(chunk * step + at)

        with_last(chunk, await_kernel)
        own_sites = pl.ds(pl.multiple_of(base * planes, half * planes), half * planes)
        top = lax.broadcasted_iota(jnp.int32, (middle, 2 * width), 0) == 0

        @pl.loop(0, step)
        def _(at):
            line = chunk * step + at
            first, second = 2 * line, 2 * line + 1
            columns = jnp.concatenate(
                [gathered[:, row].reshape(one, width) for row in (first, second)], axis=1
            )
            spectrum = from_left(ahead_ref[...], columns)
            plain = held_at(line)
            leading = (line == leading_place) & (column == 0)
            mirrored = jnp.where(leading, held_at(jnp.int32(count)), plain)
            for slot in range(slots):
                body = jnp.concatenate(
                    [kernels[plain, slot, 0:middle], kernels[mirrored, slot, 0:middle]], axis=1
                )
                edge = jnp.concatenate(
                    [
                        kernels[plain, slot, middle : middle + 1],
                        kernels[mirrored, slot, middle : middle + 1],
                    ],
                    axis=1,
                )
                factor = jnp.concatenate([body, jnp.where(top, edge, body)], axis=0)
                result = from_left(behind_ref[own_sites, :], spectrum * factor)
                product[slot, :, first] = result[:, :width].reshape(half, planes, width)
                product[slot, :, second] = result[:, width:].reshape(half, planes, width)

        for slot in range(slots):

            @pl.loop(0, half)
            def _(turn):
                receiver = base + turn

                @pl.when(receiver != me)
                def _():
                    back(slot, chunk, receiver).start()

            home(slot, chunk).start()

    pl.loop(0, lead)(send_own)

    @pl.when(inner)
    def _():
        convert()
        extra_copy(lambda copy: copy.start())

        @pl.loop(0, local)
        def _(turn):
            each_kernel_row(turn, lambda copy: copy.start())

        own.wait()

        @pl.loop(0, depth)
        def _(chunk):
            relay(chunk)
            relay_kernels(chunk)

        @pl.loop(0, chunks)
        def _(chunk):
            @pl.when(chunk + depth < chunks)
            def _():
                relay(chunk + depth)
                relay_kernels(chunk + depth)

            compute(chunk)

    @pl.when(outer)
    def _():
        pl.loop(0, early)(relay)
        convert()
        extra_copy(lambda copy: copy.start())
        late = chunks - early
        pace = -(-local // max(late, 1))

        @pl.loop(early, chunks)
        def _(chunk):
            relay(chunk)

            @pl.loop(0, pace)
            def _(at):
                turn = (chunk - early) * pace + at

                @pl.when(turn < local)
                def _():
                    each_kernel_row(turn, lambda copy: copy.start())

        if late == 0:

            @pl.loop(0, local)
            def _(turn):
                each_kernel_row(turn, lambda copy: copy.start())

    @pl.loop(0, chunks)
    def _(chunk):
        to_mate(chunk).wait_send()
        own_on(chunk).wait_send()
        pass_on(1, mate, chunk).wait_send()
        for slot in range(slots):
            back_arrival(slot, chunk, 1 - column).wait_recv()

        @pl.when(outer)
        def _():
            for slot in range(slots):
                back_arrival(slot, chunk, column).wait_recv()

        @pl.when(inner)
        def _():
            for kind, owner in ((2, behind), (3, behind_mate)):
                pass_on(kind, owner, chunk).wait_send()
            for slot in range(slots):
                home(slot, chunk).wait()

                @pl.loop(0, half)
                def _(turn):
                    receiver = base + turn

                    @pl.when(receiver != me)
                    def _():
                        back(slot, chunk, receiver).wait_send()

    @pl.loop(0, local)
    def _(turn):
        each_kernel_row(turn, lambda copy: copy.wait_send())

    extra_copy(lambda copy: copy.wait_send())

    @pl.when(inner)
    def _():
        def passed(place):
            @pl.when(arrives(place) & firsthand(place))
            def _():
                kernel_on(place).wait_send()

        pl.loop(0, count)(passed)

        @pl.when(column == 0)
        def _():
            passed(jnp.int32(count))


def second_order(length, blocks):
    count, local = length // 4, length // (2 * blocks)
    quarter = local // 2
    side, place = np.divmod(np.arange(2 * count), count)
    group, at = np.divmod(place, count // 2)
    block = 2 - 2 * group + at % 2
    value = local * block + quarter - 1 - at // 2 + quarter * side
    mirror = np.where(value == 0, length // 2, length - value)
    return np.stack([value, mirror], axis=1).reshape(-1)


def first_order(length):
    counter = np.arange(length // 2)
    return np.concatenate([counter, np.where(counter == 0, length // 2, length - counter)])


def kernel_path(adjoint, saved, spectra, chosen):
    size_px, size_py = lax.axis_size("px"), lax.axis_size("py")
    planes, lines, three = adjoint.shape
    one, two = planes * size_px, lines * size_py
    width, local, slots = three // size_py, spectra.shape[2], chosen.shape[0]
    whole = lambda table: pl.BlockSpec(table.shape, lambda *at: (0,) * table.ndim)
    anywhere = pl.BlockSpec(memory_space=pl.ANY)
    f32 = jnp.float32
    block = 8
    steps = planes // block
    dma = pltpu.SemaphoreType.DMA
    right_three = as_three(hartley(three), 0)
    half = size_px // 2
    order = second_order(two, half)
    order_one = first_order(one)
    left_two = as_three(hartley(two)[order], 1)
    left_two_back = as_three(hartley(two)[:, order], 1)
    left_one = as_three(hartley(one)[order_one], 1)
    left_one_back = as_three(hartley(one)[:, order_one], 1)

    field = pl.pallas_call(
        functools.partial(third_kernel, steps),
        grid=(steps,),
        in_specs=[pl.BlockSpec((block, lines, three), lambda i: (i, 0, 0)), whole(right_three)],
        out_specs=anywhere,
        out_shape=jax.ShapeDtypeStruct((size_py, planes, lines, width), f32),
        scratch_shapes=[pltpu.VMEM((size_py, planes, lines, width), f32)] + [dma((steps,))] * 3,
        compiler_params=params(collective_id=1, has_side_effects=True),
        name="third",
    )(adjoint, right_three)
    field = pl.pallas_call(
        second_kernel,
        grid=(planes // block,),
        in_specs=[
            pl.BlockSpec((size_py, block, lines, width), lambda i: (0, i, 0, 0)),
            whole(left_two),
        ],
        out_specs=pl.BlockSpec((2, two // 2, block, width), lambda i: (0, 0, i, 0)),
        out_shape=jax.ShapeDtypeStruct((2, two // 2, planes, width), f32),
        scratch_shapes=[pltpu.VMEM((block, two, width), f32)],
        compiler_params=params(),
        name="second",
    )(field, left_two)
    chunks = 32
    count = two // 4
    in_vmem = pl.BlockSpec(memory_space=pltpu.VMEM)
    field = pl.pallas_call(
        functools.partial(middle_kernel, chunks),
        in_specs=[anywhere, anywhere, in_vmem, in_vmem],
        out_specs=anywhere,
        out_shape=jax.ShapeDtypeStruct((slots, 2, two // 2, planes, width), f32),
        scratch_shapes=[
            pltpu.VMEM((size_px, two // 2, planes, width), f32),
            pltpu.VMEM((slots, one // 2 + 16, local, width), spectra.dtype),
            pltpu.VMEM((count + 1 + local, slots, one // 2 + 8, width), f32),
            pltpu.VMEM((slots, half, two // 2, planes, width), f32),
            dma((chunks,)),
            dma((4, chunks)),
            dma((size_px, chunks)),
            dma((local,)),
            dma((count + 1,)),
            dma((count + 1,)),
            dma,
            dma((slots, chunks, half)),
            dma((slots, chunks, 2)),
            dma((slots, chunks)),
            dma,
            dma,
        ],
        compiler_params=params(collective_id=0, has_side_effects=True),
        name="middle",
    )(field, spectra, left_one, left_one_back)
    field = pl.pallas_call(
        functools.partial(second_back_kernel, slots * steps),
        grid=(slots, steps),
        in_specs=[
            pl.BlockSpec((1, 2, two // 2, block, width), lambda j, i: (j, 0, 0, i, 0)),
            whole(left_two_back),
        ],
        out_specs=anywhere,
        out_shape=jax.ShapeDtypeStruct((size_py, slots, planes, lines, width), f32),
        scratch_shapes=[
            pltpu.VMEM((block, two, width), f32),
            pltpu.VMEM((size_py, slots, planes, lines, width), f32),
        ]
        + [dma((slots * steps,))] * 3,
        compiler_params=params(collective_id=2, has_side_effects=True),
        name="second_back",
    )(field, left_two_back)
    scale = 1.0 / (one * two * three)
    piece = 4
    return pl.pallas_call(
        functools.partial(third_back_kernel, scale),
        grid=(planes // piece,),
        in_specs=[
            pl.BlockSpec(memory_space=pltpu.SMEM),
            pl.BlockSpec((size_py, slots, piece, lines, width), lambda i: (0, 0, i, 0, 0)),
            pl.BlockSpec((piece, lines, three), lambda i: (i, 0, 0)),
            whole(right_three),
        ],
        out_specs=pl.BlockSpec((piece, lines, three), lambda i: (i, 0, 0)),
        out_shape=jax.ShapeDtypeStruct((planes, lines, three), f32),
        compiler_params=params(),
        name="third_back",
    )(chosen, field, saved, right_three)


def on_device(adjoint, saved, spectra, freq_index, picked):
    chosen = chosen_index(freq_index, picked)
    width = adjoint.shape[2] // lax.axis_size("py")
    even = lax.axis_size("px") == 8 and lax.axis_size("py") == 2 and lax.axis_size("chain") == 2
    if even and adjoint.shape[0] % 8 == 0 and spectra.shape[2] % 32 == 0 and width % 128 == 0:
        return kernel_path(adjoint, saved, spectra, chosen)
    return plain_path(adjoint, saved, spectra, chosen)


def solution(mesh):
    placed = (
        P(("chain", "px"), "py", None),
        P(("chain", "px"), "py", None),
        P(None, None, "px", None),
        P(),
        P(),
    )
    return jax.shard_map(
        on_device,
        mesh=mesh,
        in_specs=placed,
        out_specs=P(("chain", "px"), "py", None),
        check_vma=False,
    )
```

```python
import functools
import math

import jax
import jax.numpy as jnp
import numpy as np
from jax import lax
from jax.experimental import pallas as pl
from jax.experimental.pallas import tpu as pltpu
from jax.sharding import PartitionSpec as P


def hartley(length):
    counter = np.arange(length, dtype=np.int64)
    angle = (counter[:, None] * counter[None, :] % length) * (2.0 * np.pi / length)
    return np.cos(angle) + np.sin(angle)


def chosen_index(freq_index, picked):
    ids = jnp.arange(freq_index.shape[0], dtype=jnp.int32)
    return jnp.sum(jnp.where(ids[None, :] == picked[:, None], freq_index[None, :], 0), axis=1)


def along(equation, field, table):
    return jnp.einsum(equation, field, jnp.asarray(table, jnp.float32), precision=lax.Precision.HIGH)


def plain_path(adjoint, saved, spectra, chosen):
    size_px, size_py = lax.axis_size("px"), lax.axis_size("py")
    one, two, three = adjoint.shape[0] * size_px, adjoint.shape[1] * size_py, adjoint.shape[2]
    t_one, t_two, t_three = hartley(one), hartley(two), hartley(three)
    width = three // size_py
    field = along("abc,cz->abz", adjoint, t_three)
    field = lax.all_to_all(field, "py", split_axis=2, concat_axis=1, tiled=True)
    field = along("abc,bz->azc", field, t_two)
    field = lax.all_to_all(field, "px", split_axis=1, concat_axis=0, tiled=True)
    spectrum = along("abc,az->zbc", field, t_one)
    kernels = lax.dynamic_slice_in_dim(spectra, lax.axis_index("py") * width, width, 3)
    omegas = chosen.astype(jnp.float32) * (math.pi / 8.0)
    scale = 1.0 / (one * two * three)
    total = jnp.zeros(saved.shape, jnp.float32)
    for slot in range(chosen.shape[0]):
        back = along("abc,az->zbc", spectrum * kernels[slot].astype(jnp.float32), t_one)
        back = lax.all_to_all(back, "px", split_axis=0, concat_axis=1, tiled=True)
        back = along("abc,bz->azc", back, t_two)
        back = lax.all_to_all(back, "py", split_axis=1, concat_axis=2, tiled=True)
        back = along("abc,cz->abz", back, t_three) * scale
        total = total + omegas[slot] * jnp.cos(omegas[slot] * saved) * back
    return total


def as_three(matrix, axis):
    high = matrix.astype(jnp.bfloat16)
    low = (matrix - high.astype(np.float64)).astype(jnp.bfloat16)
    order = (high, high, low)
    return jnp.asarray(np.concatenate(order, axis=axis))


def split(value, axis):
    high = value.astype(jnp.bfloat16)
    low = (value - high.astype(jnp.float32)).astype(jnp.bfloat16)
    return jnp.concatenate([high, low, high], axis=axis)


def from_right(rows, table):
    return jnp.dot(split(rows, 1), table, preferred_element_type=jnp.float32)


def from_left(table, columns):
    return jnp.dot(table, split(columns, 0), preferred_element_type=jnp.float32)


def params(**more):
    return pltpu.CompilerParams(vmem_limit_bytes=58 << 20, **more)


def core_exchange(step, steps, source, target, sems):
    send_sem, recv_sem, own_sem = sems
    me = lax.axis_index("py")
    other = 1 - me

    def away(at, sender, receiver):
        return pltpu.make_async_remote_copy(
            src_ref=source(receiver, at),
            dst_ref=target(sender, at),
            send_sem=send_sem.at[at],
            recv_sem=recv_sem.at[at],
            device_id={"py": receiver},
            device_id_type=pl.DeviceIdType.MESH,
        )

    def stay(at):
        return pltpu.make_async_copy(source(me, at), target(me, at), own_sem.at[at])

    away(step, me, other).start()
    stay(step).start()

    @pl.when(step == steps - 1)
    def _():
        @pl.loop(0, steps)
        def _(at):
            away(at, me, other).wait_send()
            away(at, other, me).wait_recv()
            stay(at).wait()


def greet_core():
    barrier = pltpu.get_barrier_semaphore()
    other = 1 - lax.axis_index("py")
    pl.semaphore_signal(
        barrier, inc=1, device_id={"py": other}, device_id_type=pl.DeviceIdType.MESH
    )
    pl.semaphore_wait(barrier, 1)


def third_kernel(steps, field_ref, table_ref, out_ref, mine, *sems):
    planes, lines, three = field_ref.shape
    parts, width = mine.shape[0], mine.shape[3]
    step = pl.program_id(0)
    pl.when(step == 0)(greet_core)

    def rows(at):
        return pl.ds(pl.multiple_of(at * planes, planes), planes)

    result = from_right(field_ref[...].reshape(planes * lines, three), table_ref[...])
    for part in range(parts):
        piece = result[:, part * width : (part + 1) * width]
        mine[part, rows(step)] = piece.reshape(planes, lines, width)
    core_exchange(
        step,
        steps,
        lambda part, at: mine.at[part, rows(at)],
        lambda part, at: out_ref.at[part, rows(at)],
        sems,
    )


def second_kernel(field_ref, table_ref, out_ref, held):
    parts, planes, _, width = field_ref.shape
    size_px, local, _, _ = out_ref.shape
    for plane in range(0, planes, 2):
        sides = [
            jnp.concatenate([field_ref[part, at] for part in range(parts)], axis=0)
            for at in (plane, plane + 1)
        ]
        result = from_left(table_ref[...], jnp.concatenate(sides, axis=1))
        held[plane] = result[:, :width]
        held[plane + 1] = result[:, width:]
    for peer in range(size_px):
        out_ref[peer] = jnp.swapaxes(held[:, peer * local : (peer + 1) * local, :], 0, 1)


def second_back_kernel(steps, field_ref, table_ref, out_ref, held, mine, *sems):
    _, groups, local, planes, width = field_ref.shape
    parts, lines = mine.shape[0], mine.shape[3]
    inner = steps // mine.shape[1]
    step = pl.program_id(0) * inner + pl.program_id(1)
    slot = pl.program_id(0)
    begin = pl.program_id(1) * planes
    pl.when(step == 0)(greet_core)
    for group in range(groups):
        held[:, group * local : (group + 1) * local, :] = jnp.swapaxes(field_ref[0, group], 0, 1)
    for plane in range(0, planes, 2):
        columns = jnp.concatenate([held[plane], held[plane + 1]], axis=1)
        result = from_left(table_ref[...], columns)
        for part in range(parts):
            rows = result[part * lines : (part + 1) * lines]
            mine[part, slot, begin + plane] = rows[:, :width]
            mine[part, slot, begin + plane + 1] = rows[:, width:]

    def block(ref):
        return lambda part, at: ref.at[part, at // inner, pl.ds((at % inner) * planes, planes)]

    core_exchange(step, steps, block(mine), block(out_ref), sems)


def cosine_turns(turns):
    turns = turns - jnp.floor(turns + 0.5)
    square = turns * turns * (4.0 * math.pi * math.pi)
    value = jnp.full_like(square, 1.0 / math.factorial(20))
    for order in range(9, -1, -1):
        value = value * square + (-1.0) ** order / math.factorial(2 * order)
    return value


def third_back_kernel(scale, chosen_ref, field_ref, saved_ref, table_ref, out_ref):
    parts, slots, planes, lines, width = field_ref.shape
    three = parts * width
    total = None
    site = saved_ref[...].reshape(planes * lines, three)
    for slot in range(slots):
        sides = [field_ref[part, slot].reshape(planes * lines, width) for part in range(parts)]
        field = from_right(jnp.concatenate(sides, axis=1), table_ref[...])
        index = chosen_ref[slot].astype(jnp.float32)
        weight = cosine_turns(site * (index * (1.0 / 16.0))) * (index * (math.pi / 8.0 * scale))
        total = weight * field if total is None else total + weight * field
    out_ref[...] = total.reshape(planes, lines, three)


def middle_kernel(
    chunks,
    field_ref,
    spectra_ref,
    ahead_ref,
    behind_ref,
    out_ref,
    gathered,
    raw,
    kernels,
    product,
    mate_send,
    next_send,
    go_recv,
    kernel_send,
    kernel_recv,
    kernel_pass,
    extra_send,
    back_send,
    back_recv,
    home_sem,
    own_sem,
    raw_sem,
):
    _, rows_all, planes, width = field_ref.shape
    size_px, slots = gathered.shape[0], raw.shape[0]
    half, count = size_px // 2, rows_all // 2
    held_rows, local = raw.shape[1], raw.shape[2]
    one, middle, quarter = size_px * planes, size_px * planes // 2, local // 2
    two = size_px * local
    step = count // chunks
    lead, depth, early = 2, 1, min(10, chunks // 2)
    per_chunk = -(-2 * local // chunks)
    first_rows = min(local, 4 * per_chunk)
    pace = -(-local // (chunks - early)) + 0
    me = lax.axis_index("px")
    part = lax.axis_index("py")
    turn_of = lax.axis_index("chain")
    lower = me < half
    base = jnp.where(lower, 0, half)
    column = lax.rem(me, 2)
    mate = me + 1 - 2 * column
    onward = jnp.where(lower, me + 2, me - 2)
    behind = jnp.where(lower, me - 2, me + 2)
    behind_mate = behind + 1 - 2 * column
    inner = (me >= half - 2) & (me < half + 2)
    outer = jnp.logical_not(inner)
    centre = jnp.where(lower, half - 2, half)

    def to(index):
        return dict(device_id={"px": index}, device_id_type=pl.DeviceIdType.MESH)

    def across():
        return dict(device_id={"chain": 1 - turn_of}, device_id_type=pl.DeviceIdType.MESH)

    def rows(chunk):
        return pl.ds(pl.multiple_of(chunk * 2 * step, 2 * step), 2 * step)

    def to_mate(chunk):
        return pltpu.make_async_remote_copy(
            src_ref=field_ref.at[1 - column, rows(chunk)],
            dst_ref=gathered.at[me, rows(chunk)],
            send_sem=mate_send.at[chunk],
            recv_sem=go_recv.at[me, chunk],
            **to(mate),
        )

    def own_on(chunk):
        return pltpu.make_async_remote_copy(
            src_ref=field_ref.at[column, rows(chunk)],
            dst_ref=gathered.at[me, rows(chunk)],
            send_sem=next_send.at[0, chunk],
            recv_sem=go_recv.at[me, chunk],
            **to(onward),
        )

    def pass_on(kind, owner, chunk):
        return pltpu.make_async_remote_copy(
            src_ref=gathered.at[owner, rows(chunk)],
            dst_ref=gathered.at[owner, rows(chunk)],
            send_sem=next_send.at[kind, chunk],
            recv_sem=go_recv.at[owner, chunk],
            **to(onward),
        )

    def back(slot, chunk, receiver):
        return pltpu.make_async_remote_copy(
            src_ref=product.at[slot, receiver - base, rows(chunk)],
            dst_ref=out_ref.at[slot, column, rows(chunk)],
            send_sem=back_send.at[slot, chunk, receiver - base],
            recv_sem=back_recv.at[slot, chunk, column],
            **to(receiver),
        )

    def back_arrival(slot, chunk, side):
        return pltpu.make_async_remote_copy(
            src_ref=product.at[slot, 0, rows(chunk)],
            dst_ref=out_ref.at[slot, side, rows(chunk)],
            send_sem=back_send.at[slot, chunk, 0],
            recv_sem=back_recv.at[slot, chunk, side],
            **to(mate),
        )

    def home(slot, chunk):
        return pltpu.make_async_copy(
            product.at[slot, me - base, rows(chunk)],
            out_ref.at[slot, column, rows(chunk)],
            home_sem.at[slot, chunk],
        )

    def frequency(place):
        group, at = lax.div(place, count // 2), lax.rem(place, count // 2)
        block = 2 - 2 * group + lax.rem(at, 2)
        return local * block + quarter - 1 - lax.div(at, 2) + quarter * column

    def source(place):
        value = jnp.where(place == count, two // 2, frequency(place))
        above = jnp.where(value == 0, 0, lax.div(two - value, local))
        holder = jnp.where(lower, lax.div(value, local), above)
        row = jnp.where(lower | (value == 0), lax.rem(value, local), lax.rem(two - value, local))
        return jnp.where(place == count, half, holder), row

    def held_at(place):
        holder, row = source(place)
        return jnp.where(holder == me, count + 1 + row, place)

    def firsthand(place):
        return lax.rem(lax.div(place, 2), 2) == turn_of

    def kernel_row(turn):
        turn = jnp.where(lower, turn, lax.rem(turn + local - 2, local))
        offset = quarter - 1 - lax.div(turn, 2) + quarter * lax.rem(turn, 2)
        row = jnp.where(lower, offset, lax.rem(local - offset, local))
        value = jnp.where(lower, local * me + row, two - local * me - row)
        block, inside = lax.div(value, local), lax.rem(value, local)
        side, level = lax.div(inside, quarter), lax.rem(inside, quarter)
        place = jnp.where(block >= 2, 0, count // 2) + 2 * (quarter - 1 - level) + lax.rem(block, 2)
        return row, side, jnp.where(value == two // 2, count, place)

    def kernel_copy(row, place, receiver, sem):
        return pltpu.make_async_remote_copy(
            src_ref=kernels.at[count + 1 + row],
            dst_ref=kernels.at[place],
            send_sem=sem,
            recv_sem=kernel_recv.at[place],
            **to(receiver),
        )

    def each_kernel_row(turn, act):
        row, side, place = kernel_row(turn)

        @pl.when((centre + side != me) & firsthand(place))
        def _():
            act(kernel_copy(row, place, centre + side, kernel_send.at[row]))

    def extra_copy(act):
        for sender, place, receiver in ((0, count - 2, half), (half, count, half - 2)):

            @pl.when((me == sender) & firsthand(jnp.int32(place)))
            def _():
                act(kernel_copy(0, place, jnp.int32(receiver), extra_send))

    def kernel_arrival(place):
        return kernel_copy(0, place, mate, extra_send)

    def kernel_on(place):
        return pltpu.make_async_remote_copy(
            src_ref=kernels.at[place],
            dst_ref=kernels.at[place],
            send_sem=kernel_pass.at[place],
            recv_sem=kernel_recv.at[place],
            **across(),
        )

    def arrives(place):
        return source(place)[0] != me

    leading_place = count - 2

    def pass_kernel(place):
        @pl.when(arrives(place) & firsthand(place))
        def _():
            kernel_arrival(place).wait_recv()
            kernel_on(place).start()

    def await_kernel(place):
        @pl.when(arrives(place) & jnp.logical_not(firsthand(place)))
        def _():
            kernel_arrival(place).wait_recv()

    def with_last(chunk, act):
        @pl.when((chunk == leading_place // step) & (column == 0))
        def _():
            act(jnp.int32(count))

    own = pltpu.make_async_copy(field_ref.at[column], gathered.at[me], own_sem)
    fetch = pltpu.make_async_copy(
        spectra_ref.at[:, pl.ds(0, held_rows), :, pl.ds(part * width, width)], raw, raw_sem
    )
    fetch.start()

    @pl.when(inner)
    def _():
        own.start()

    barrier = pltpu.get_barrier_semaphore()
    everyone = 2 * size_px

    @pl.loop(1, everyone)
    def _(turn):
        peer = lax.rem(turn_of * size_px + me + turn, everyone)
        pl.semaphore_signal(
            barrier,
            inc=1,
            device_id={"chain": lax.div(peer, size_px), "px": lax.rem(peer, size_px)},
            device_id_type=pl.DeviceIdType.MESH,
        )

    pl.semaphore_wait(barrier, everyone - 1)

    def send_own(chunk):
        own_on(chunk).start()
        to_mate(chunk).start()

    def convert():
        fetch.wait()
        block = 16
        for slot in range(slots):

            @pl.loop(0, middle // block)
            def _(at):
                span = pl.ds(pl.multiple_of(at * block, block), block)
                piece = raw[slot, span].astype(jnp.float32)
                kernels[count + 1 :, slot, span, :] = jnp.swapaxes(piece, 0, 1)

            piece = raw[slot, middle : middle + block].astype(jnp.float32)
            kernels[count + 1 :, slot, middle : middle + 8, :] = jnp.swapaxes(piece[:8], 0, 1)

    def relay(chunk):
        pass_on(1, mate, chunk).wait_recv()
        pass_on(1, mate, chunk).start()

        @pl.when(inner)
        def _():
            for kind, owner in ((2, behind), (3, behind_mate)):
                pass_on(kind, owner, chunk).wait_recv()
                pass_on(kind, owner, chunk).start()

        @pl.when(chunk + lead < chunks)
        def _():
            send_own(chunk + lead)

    def relay_kernels(chunk):
        @pl.loop(0, step)
        def _(at):
            pass_kernel(chunk * step + at)

        with_last(chunk, pass_kernel)

    def compute(chunk):
        for owner in (onward, onward + 1 - 2 * column):
            pass_on(1, owner, chunk).wait_recv()
        further = jnp.where(lower, onward + 2, onward - 2)
        for owner in (further, further + 1 - 2 * column):
            pass_on(1, owner, chunk).wait_recv()

        @pl.loop(0, step)
        def _(at):
            await_kernel(chunk * step + at)

        with_last(chunk, await_kernel)
        own_sites = pl.ds(pl.multiple_of(base * planes, half * planes), half * planes)
        top = lax.broadcasted_iota(jnp.int32, (middle, 2 * width), 0) == 0

        @pl.loop(0, step)
        def _(at):
            line = chunk * step + at
            first, second = 2 * line, 2 * line + 1
            columns = jnp.concatenate(
                [gathered[:, row].reshape(one, width) for row in (first, second)], axis=1
            )
            spectrum = from_left(ahead_ref[...], columns)
            plain = held_at(line)
            leading = (line == leading_place) & (column == 0)
            mirrored = jnp.where(leading, held_at(jnp.int32(count)), plain)
            for slot in range(slots):
                body = jnp.concatenate(
                    [kernels[plain, slot, 0:middle], kernels[mirrored, slot, 0:middle]], axis=1
                )
                edge = jnp.concatenate(
                    [
                        kernels[plain, slot, middle : middle + 1],
                        kernels[mirrored, slot, middle : middle + 1],
                    ],
                    axis=1,
                )
                factor = jnp.concatenate([body, jnp.where(top, edge, body)], axis=0)
                result = from_left(behind_ref[own_sites, :], spectrum * factor)
                product[slot, :, first] = result[:, :width].reshape(half, planes, width)
                product[slot, :, second] = result[:, width:].reshape(half, planes, width)

        for slot in range(slots):

            @pl.loop(0, half)
            def _(turn):
                receiver = base + turn

                @pl.when(receiver != me)
                def _():
                    back(slot, chunk, receiver).start()

            home(slot, chunk).start()

    def send_kernels(begin, length):
        @pl.loop(0, length)
        def _(at):
            @pl.when(begin + at < local)
            def _():
                each_kernel_row(begin + at, lambda copy: copy.start())

    pl.loop(0, lead)(send_own)

    @pl.when(inner)
    def _():
        convert()
        extra_copy(lambda copy: copy.start())

        send_kernels(jnp.int32(0), first_rows)
        own.wait()

        @pl.loop(0, depth)
        def _(chunk):
            relay(chunk)
            relay_kernels(chunk)

        @pl.loop(0, chunks)
        def _(chunk):
            send_kernels(first_rows + chunk * per_chunk, per_chunk)

            @pl.when(chunk + depth < chunks)
            def _():
                relay(chunk + depth)
                relay_kernels(chunk + depth)

            compute(chunk)

    @pl.when(outer)
    def _():
        pl.loop(0, early)(relay)
        convert()
        extra_copy(lambda copy: copy.start())

        @pl.loop(early, chunks)
        def _(chunk):
            relay(chunk)
            send_kernels((chunk - early) * pace, pace)

    @pl.loop(0, chunks)
    def _(chunk):
        to_mate(chunk).wait_send()
        own_on(chunk).wait_send()
        pass_on(1, mate, chunk).wait_send()
        for slot in range(slots):
            back_arrival(slot, chunk, 1 - column).wait_recv()

        @pl.when(outer)
        def _():
            for slot in range(slots):
                back_arrival(slot, chunk, column).wait_recv()

        @pl.when(inner)
        def _():
            for kind, owner in ((2, behind), (3, behind_mate)):
                pass_on(kind, owner, chunk).wait_send()
            for slot in range(slots):
                home(slot, chunk).wait()

                @pl.loop(0, half)
                def _(turn):
                    receiver = base + turn

                    @pl.when(receiver != me)
                    def _():
                        back(slot, chunk, receiver).wait_send()

    @pl.loop(0, local)
    def _(turn):
        each_kernel_row(turn, lambda copy: copy.wait_send())

    extra_copy(lambda copy: copy.wait_send())

    @pl.when(inner)
    def _():
        def passed(place):
            @pl.when(arrives(place) & firsthand(place))
            def _():
                kernel_on(place).wait_send()

        pl.loop(0, count)(passed)

        @pl.when(column == 0)
        def _():
            passed(jnp.int32(count))


def second_order(length, blocks):
    count, local = length // 4, length // (2 * blocks)
    quarter = local // 2
    side, place = np.divmod(np.arange(2 * count), count)
    group, at = np.divmod(place, count // 2)
    block = 2 - 2 * group + at % 2
    value = local * block + quarter - 1 - at // 2 + quarter * side
    mirror = np.where(value == 0, length // 2, length - value)
    return np.stack([value, mirror], axis=1).reshape(-1)


def first_order(length):
    counter = np.arange(length // 2)
    return np.concatenate([counter, np.where(counter == 0, length // 2, length - counter)])


def kernel_path(adjoint, saved, spectra, chosen):
    size_px, size_py = lax.axis_size("px"), lax.axis_size("py")
    planes, lines, three = adjoint.shape
    one, two = planes * size_px, lines * size_py
    width, local, slots = three // size_py, spectra.shape[2], chosen.shape[0]
    whole = lambda table: pl.BlockSpec(table.shape, lambda *at: (0,) * table.ndim)
    anywhere = pl.BlockSpec(memory_space=pl.ANY)
    f32 = jnp.float32
    block = 8
    steps = planes // block
    dma = pltpu.SemaphoreType.DMA
    right_three = as_three(hartley(three), 0)
    half = size_px // 2
    order = second_order(two, half)
    order_one = first_order(one)
    left_two = as_three(hartley(two)[order], 1)
    left_two_back = as_three(hartley(two)[:, order], 1)
    left_one = as_three(hartley(one)[order_one], 1)
    left_one_back = as_three(hartley(one)[:, order_one], 1)

    field = pl.pallas_call(
        functools.partial(third_kernel, steps),
        grid=(steps,),
        in_specs=[pl.BlockSpec((block, lines, three), lambda i: (i, 0, 0)), whole(right_three)],
        out_specs=anywhere,
        out_shape=jax.ShapeDtypeStruct((size_py, planes, lines, width), f32),
        scratch_shapes=[pltpu.VMEM((size_py, planes, lines, width), f32)] + [dma((steps,))] * 3,
        compiler_params=params(collective_id=1, has_side_effects=True),
        name="third",
    )(adjoint, right_three)
    field = pl.pallas_call(
        second_kernel,
        grid=(planes // block,),
        in_specs=[
            pl.BlockSpec((size_py, block, lines, width), lambda i: (0, i, 0, 0)),
            whole(left_two),
        ],
        out_specs=pl.BlockSpec((2, two // 2, block, width), lambda i: (0, 0, i, 0)),
        out_shape=jax.ShapeDtypeStruct((2, two // 2, planes, width), f32),
        scratch_shapes=[pltpu.VMEM((block, two, width), f32)],
        compiler_params=params(),
        name="second",
    )(field, left_two)
    chunks = 32
    count = two // 4
    in_vmem = pl.BlockSpec(memory_space=pltpu.VMEM)
    field = pl.pallas_call(
        functools.partial(middle_kernel, chunks),
        in_specs=[anywhere, anywhere, in_vmem, in_vmem],
        out_specs=anywhere,
        out_shape=jax.ShapeDtypeStruct((slots, 2, two // 2, planes, width), f32),
        scratch_shapes=[
            pltpu.VMEM((size_px, two // 2, planes, width), f32),
            pltpu.VMEM((slots, one // 2 + 16, local, width), spectra.dtype),
            pltpu.VMEM((count + 1 + local, slots, one // 2 + 8, width), f32),
            pltpu.VMEM((slots, half, two // 2, planes, width), f32),
            dma((chunks,)),
            dma((4, chunks)),
            dma((size_px, chunks)),
            dma((local,)),
            dma((count + 1,)),
            dma((count + 1,)),
            dma,
            dma((slots, chunks, half)),
            dma((slots, chunks, 2)),
            dma((slots, chunks)),
            dma,
            dma,
        ],
        compiler_params=params(collective_id=0, has_side_effects=True),
        name="middle",
    )(field, spectra, left_one, left_one_back)
    field = pl.pallas_call(
        functools.partial(second_back_kernel, slots * steps),
        grid=(slots, steps),
        in_specs=[
            pl.BlockSpec((1, 2, two // 2, block, width), lambda j, i: (j, 0, 0, i, 0)),
            whole(left_two_back),
        ],
        out_specs=anywhere,
        out_shape=jax.ShapeDtypeStruct((size_py, slots, planes, lines, width), f32),
        scratch_shapes=[
            pltpu.VMEM((block, two, width), f32),
            pltpu.VMEM((size_py, slots, planes, lines, width), f32),
        ]
        + [dma((slots * steps,))] * 3,
        compiler_params=params(collective_id=2, has_side_effects=True),
        name="second_back",
    )(field, left_two_back)
    scale = 1.0 / (one * two * three)
    piece = 4
    return pl.pallas_call(
        functools.partial(third_back_kernel, scale),
        grid=(planes // piece,),
        in_specs=[
            pl.BlockSpec(memory_space=pltpu.SMEM),
            pl.BlockSpec((size_py, slots, piece, lines, width), lambda i: (0, 0, i, 0, 0)),
            pl.BlockSpec((piece, lines, three), lambda i: (i, 0, 0)),
            whole(right_three),
        ],
        out_specs=pl.BlockSpec((piece, lines, three), lambda i: (i, 0, 0)),
        out_shape=jax.ShapeDtypeStruct((planes, lines, three), f32),
        compiler_params=params(),
        name="third_back",
    )(chosen, field, saved, right_three)


def on_device(adjoint, saved, spectra, freq_index, picked):
    chosen = chosen_index(freq_index, picked)
    width = adjoint.shape[2] // lax.axis_size("py")
    even = lax.axis_size("px") == 8 and lax.axis_size("py") == 2 and lax.axis_size("chain") == 2
    if even and adjoint.shape[0] % 8 == 0 and spectra.shape[2] % 32 == 0 and width % 128 == 0:
        return kernel_path(adjoint, saved, spectra, chosen)
    return plain_path(adjoint, saved, spectra, chosen)


def solution(mesh):
    placed = (
        P(("chain", "px"), "py", None),
        P(("chain", "px"), "py", None),
        P(None, None, "px", None),
        P(),
        P(),
    )
    return jax.shard_map(
        on_device,
        mesh=mesh,
        in_specs=placed,
        out_specs=P(("chain", "px"), "py", None),
        check_vma=False,
    )
```

```python
import functools
import math

import jax
import jax.numpy as jnp
import numpy as np
from jax import lax
from jax.experimental import pallas as pl
from jax.experimental.pallas import tpu as pltpu
from jax.sharding import PartitionSpec as P


def hartley(length):
    counter = np.arange(length, dtype=np.int64)
    angle = (counter[:, None] * counter[None, :] % length) * (2.0 * np.pi / length)
    return np.cos(angle) + np.sin(angle)


def chosen_index(freq_index, picked):
    ids = jnp.arange(freq_index.shape[0], dtype=jnp.int32)
    return jnp.sum(jnp.where(ids[None, :] == picked[:, None], freq_index[None, :], 0), axis=1)


def along(equation, field, table):
    return jnp.einsum(equation, field, jnp.asarray(table, jnp.float32), precision=lax.Precision.HIGH)


def plain_path(adjoint, saved, spectra, chosen):
    size_px, size_py = lax.axis_size("px"), lax.axis_size("py")
    one, two, three = adjoint.shape[0] * size_px, adjoint.shape[1] * size_py, adjoint.shape[2]
    t_one, t_two, t_three = hartley(one), hartley(two), hartley(three)
    width = three // size_py
    field = along("abc,cz->abz", adjoint, t_three)
    field = lax.all_to_all(field, "py", split_axis=2, concat_axis=1, tiled=True)
    field = along("abc,bz->azc", field, t_two)
    field = lax.all_to_all(field, "px", split_axis=1, concat_axis=0, tiled=True)
    spectrum = along("abc,az->zbc", field, t_one)
    kernels = lax.dynamic_slice_in_dim(spectra, lax.axis_index("py") * width, width, 3)
    omegas = chosen.astype(jnp.float32) * (math.pi / 8.0)
    scale = 1.0 / (one * two * three)
    total = jnp.zeros(saved.shape, jnp.float32)
    for slot in range(chosen.shape[0]):
        back = along("abc,az->zbc", spectrum * kernels[slot].astype(jnp.float32), t_one)
        back = lax.all_to_all(back, "px", split_axis=0, concat_axis=1, tiled=True)
        back = along("abc,bz->azc", back, t_two)
        back = lax.all_to_all(back, "py", split_axis=1, concat_axis=2, tiled=True)
        back = along("abc,cz->abz", back, t_three) * scale
        total = total + omegas[slot] * jnp.cos(omegas[slot] * saved) * back
    return total


def as_three(matrix, axis):
    high = matrix.astype(jnp.bfloat16)
    low = (matrix - high.astype(np.float64)).astype(jnp.bfloat16)
    order = (high, high, low)
    return jnp.asarray(np.concatenate(order, axis=axis))


def split(value, axis):
    high = value.astype(jnp.bfloat16)
    low = (value - high.astype(jnp.float32)).astype(jnp.bfloat16)
    return jnp.concatenate([high, low, high], axis=axis)


def from_right(rows, table):
    return jnp.dot(split(rows, 1), table, preferred_element_type=jnp.float32)


def from_left(table, columns):
    return jnp.dot(table, split(columns, 0), preferred_element_type=jnp.float32)


def params(**more):
    return pltpu.CompilerParams(vmem_limit_bytes=58 << 20, **more)


def core_exchange(step, steps, source, target, sems):
    send_sem, recv_sem, own_sem = sems
    me = lax.axis_index("py")
    other = 1 - me

    def away(at, sender, receiver):
        return pltpu.make_async_remote_copy(
            src_ref=source(receiver, at),
            dst_ref=target(sender, at),
            send_sem=send_sem.at[at],
            recv_sem=recv_sem.at[at],
            device_id={"py": receiver},
            device_id_type=pl.DeviceIdType.MESH,
        )

    def stay(at):
        return pltpu.make_async_copy(source(me, at), target(me, at), own_sem.at[at])

    away(step, me, other).start()
    stay(step).start()

    @pl.when(step == steps - 1)
    def _():
        @pl.loop(0, steps)
        def _(at):
            away(at, me, other).wait_send()
            away(at, other, me).wait_recv()
            stay(at).wait()


def greet_core():
    barrier = pltpu.get_barrier_semaphore()
    other = 1 - lax.axis_index("py")
    pl.semaphore_signal(
        barrier, inc=1, device_id={"py": other}, device_id_type=pl.DeviceIdType.MESH
    )
    pl.semaphore_wait(barrier, 1)


def third_kernel(steps, field_ref, table_ref, out_ref, mine, *sems):
    planes, lines, three = field_ref.shape
    parts, width = mine.shape[0], mine.shape[3]
    step = pl.program_id(0)
    pl.when(step == 0)(greet_core)

    def rows(at):
        return pl.ds(pl.multiple_of(at * planes, planes), planes)

    result = from_right(field_ref[...].reshape(planes * lines, three), table_ref[...])
    for part in range(parts):
        piece = result[:, part * width : (part + 1) * width]
        mine[part, rows(step)] = piece.reshape(planes, lines, width)
    core_exchange(
        step,
        steps,
        lambda part, at: mine.at[part, rows(at)],
        lambda part, at: out_ref.at[part, rows(at)],
        sems,
    )


def second_kernel(field_ref, table_ref, out_ref, held):
    parts, planes, _, width = field_ref.shape
    size_px, local, _, _ = out_ref.shape
    for plane in range(0, planes, 2):
        sides = [
            jnp.concatenate([field_ref[part, at] for part in range(parts)], axis=0)
            for at in (plane, plane + 1)
        ]
        result = from_left(table_ref[...], jnp.concatenate(sides, axis=1))
        held[plane] = result[:, :width]
        held[plane + 1] = result[:, width:]
    for peer in range(size_px):
        out_ref[peer] = jnp.swapaxes(held[:, peer * local : (peer + 1) * local, :], 0, 1)


def cosine_turns(turns):
    turns = turns - jnp.floor(turns + 0.5)
    square = turns * turns * (4.0 * math.pi * math.pi)
    value = jnp.full_like(square, 1.0 / math.factorial(20))
    for order in range(9, -1, -1):
        value = value * square + (-1.0) ** order / math.factorial(2 * order)
    return value


def second_back_kernel(steps, field_ref, table_ref, out_ref, held, mine, *sems):
    _, groups, local, planes, width = field_ref.shape
    parts, lines = mine.shape[0], mine.shape[3]
    inner = steps // mine.shape[1]
    step = pl.program_id(0) * inner + pl.program_id(1)
    slot = pl.program_id(0)
    begin = pl.program_id(1) * planes
    pl.when(step == 0)(greet_core)
    for group in range(groups):
        held[:, group * local : (group + 1) * local, :] = jnp.swapaxes(field_ref[0, group], 0, 1)
    for plane in range(0, planes, 2):
        columns = jnp.concatenate([held[plane], held[plane + 1]], axis=1)
        result = from_left(table_ref[...], columns)
        for part in range(parts):
            rows = result[part * lines : (part + 1) * lines]
            mine[part, slot, begin + plane] = rows[:, :width]
            mine[part, slot, begin + plane + 1] = rows[:, width:]

    def block(ref):
        return lambda part, at: ref.at[part, at // inner, pl.ds((at % inner) * planes, planes)]

    core_exchange(step, steps, block(mine), block(out_ref), sems)


def third_back_kernel(field_ref, weight_ref, table_ref, out_ref):
    parts, slots, planes, lines, width = field_ref.shape
    three = parts * width
    total = None
    for slot in range(slots):
        sides = [field_ref[part, slot].reshape(planes * lines, width) for part in range(parts)]
        field = from_right(jnp.concatenate(sides, axis=1), table_ref[...])
        term = weight_ref[slot].reshape(planes * lines, three) * field
        total = term if total is None else total + term
    out_ref[...] = total.reshape(planes, lines, three)


def middle_kernel(
    chunks,
    scale,
    chosen_ref,
    field_ref,
    spectra_ref,
    saved_ref,
    ahead_ref,
    behind_ref,
    out_ref,
    weight_ref,
    site,
    weighed,
    gathered,
    raw,
    kernels,
    product,
    mate_send,
    next_send,
    go_recv,
    kernel_send,
    kernel_recv,
    kernel_pass,
    extra_send,
    back_send,
    back_recv,
    home_sem,
    own_sem,
    raw_sem,
    site_sem,
    weigh_sem,
):
    _, rows_all, planes, width = field_ref.shape
    size_px, slots = gathered.shape[0], raw.shape[0]
    half, count = size_px // 2, rows_all // 2
    held_rows, local = raw.shape[1], raw.shape[2]
    one, middle, quarter = size_px * planes, size_px * planes // 2, local // 2
    two = size_px * local
    step = count // chunks
    lead, depth, early = 2, 1, min(10, chunks // 2)
    per_chunk = -(-2 * local // chunks)
    first_rows = min(local, 4 * per_chunk)
    pace = -(-local // (chunks - early)) + 0
    me = lax.axis_index("px")
    part = lax.axis_index("py")
    turn_of = lax.axis_index("chain")
    lower = me < half
    base = jnp.where(lower, 0, half)
    column = lax.rem(me, 2)
    mate = me + 1 - 2 * column
    onward = jnp.where(lower, me + 2, me - 2)
    behind = jnp.where(lower, me - 2, me + 2)
    behind_mate = behind + 1 - 2 * column
    inner = (me >= half - 2) & (me < half + 2)
    outer = jnp.logical_not(inner)
    centre = jnp.where(lower, half - 2, half)

    def to(index):
        return dict(device_id={"px": index}, device_id_type=pl.DeviceIdType.MESH)

    def across():
        return dict(device_id={"chain": 1 - turn_of}, device_id_type=pl.DeviceIdType.MESH)

    def rows(chunk):
        return pl.ds(pl.multiple_of(chunk * 2 * step, 2 * step), 2 * step)

    def to_mate(chunk):
        return pltpu.make_async_remote_copy(
            src_ref=field_ref.at[1 - column, rows(chunk)],
            dst_ref=gathered.at[me, rows(chunk)],
            send_sem=mate_send.at[chunk],
            recv_sem=go_recv.at[me, chunk],
            **to(mate),
        )

    def own_on(chunk):
        return pltpu.make_async_remote_copy(
            src_ref=field_ref.at[column, rows(chunk)],
            dst_ref=gathered.at[me, rows(chunk)],
            send_sem=next_send.at[0, chunk],
            recv_sem=go_recv.at[me, chunk],
            **to(onward),
        )

    def pass_on(kind, owner, chunk):
        return pltpu.make_async_remote_copy(
            src_ref=gathered.at[owner, rows(chunk)],
            dst_ref=gathered.at[owner, rows(chunk)],
            send_sem=next_send.at[kind, chunk],
            recv_sem=go_recv.at[owner, chunk],
            **to(onward),
        )

    def back(slot, chunk, receiver):
        return pltpu.make_async_remote_copy(
            src_ref=product.at[slot, receiver - base, rows(chunk)],
            dst_ref=out_ref.at[slot, column, rows(chunk)],
            send_sem=back_send.at[slot, chunk, receiver - base],
            recv_sem=back_recv.at[slot, chunk, column],
            **to(receiver),
        )

    def back_arrival(slot, chunk, side):
        return pltpu.make_async_remote_copy(
            src_ref=product.at[slot, 0, rows(chunk)],
            dst_ref=out_ref.at[slot, side, rows(chunk)],
            send_sem=back_send.at[slot, chunk, 0],
            recv_sem=back_recv.at[slot, chunk, side],
            **to(mate),
        )

    def home(slot, chunk):
        return pltpu.make_async_copy(
            product.at[slot, me - base, rows(chunk)],
            out_ref.at[slot, column, rows(chunk)],
            home_sem.at[slot, chunk],
        )

    def frequency(place):
        group, at = lax.div(place, count // 2), lax.rem(place, count // 2)
        block = 2 - 2 * group + lax.rem(at, 2)
        return local * block + quarter - 1 - lax.div(at, 2) + quarter * column

    def source(place):
        value = jnp.where(place == count, two // 2, frequency(place))
        above = jnp.where(value == 0, 0, lax.div(two - value, local))
        holder = jnp.where(lower, lax.div(value, local), above)
        row = jnp.where(lower | (value == 0), lax.rem(value, local), lax.rem(two - value, local))
        return jnp.where(place == count, half, holder), row

    def held_at(place):
        holder, row = source(place)
        return jnp.where(holder == me, count + 1 + row, place)

    def firsthand(place):
        return lax.rem(lax.div(place, 2), 2) == turn_of

    def kernel_row(turn):
        turn = jnp.where(lower, turn, lax.rem(turn + local - 2, local))
        offset = quarter - 1 - lax.div(turn, 2) + quarter * lax.rem(turn, 2)
        row = jnp.where(lower, offset, lax.rem(local - offset, local))
        value = jnp.where(lower, local * me + row, two - local * me - row)
        block, inside = lax.div(value, local), lax.rem(value, local)
        side, level = lax.div(inside, quarter), lax.rem(inside, quarter)
        place = jnp.where(block >= 2, 0, count // 2) + 2 * (quarter - 1 - level) + lax.rem(block, 2)
        return row, side, jnp.where(value == two // 2, count, place)

    def kernel_copy(row, place, receiver, sem):
        return pltpu.make_async_remote_copy(
            src_ref=kernels.at[count + 1 + row],
            dst_ref=kernels.at[place],
            send_sem=sem,
            recv_sem=kernel_recv.at[place],
            **to(receiver),
        )

    def each_kernel_row(turn, act):
        row, side, place = kernel_row(turn)

        @pl.when((centre + side != me) & firsthand(place))
        def _():
            act(kernel_copy(row, place, centre + side, kernel_send.at[row]))

    def extra_copy(act):
        for sender, place, receiver in ((0, count - 2, half), (half, count, half - 2)):

            @pl.when((me == sender) & firsthand(jnp.int32(place)))
            def _():
                act(kernel_copy(0, place, jnp.int32(receiver), extra_send))

    def kernel_arrival(place):
        return kernel_copy(0, place, mate, extra_send)

    def kernel_on(place):
        return pltpu.make_async_remote_copy(
            src_ref=kernels.at[place],
            dst_ref=kernels.at[place],
            send_sem=kernel_pass.at[place],
            recv_sem=kernel_recv.at[place],
            **across(),
        )

    def arrives(place):
        return source(place)[0] != me

    leading_place = count - 2

    def pass_kernel(place):
        @pl.when(arrives(place) & firsthand(place))
        def _():
            kernel_arrival(place).wait_recv()
            kernel_on(place).start()

    def await_kernel(place):
        @pl.when(arrives(place) & jnp.logical_not(firsthand(place)))
        def _():
            kernel_arrival(place).wait_recv()

    def with_last(chunk, act):
        @pl.when((chunk == leading_place // step) & (column == 0))
        def _():
            act(jnp.int32(count))

    own = pltpu.make_async_copy(field_ref.at[column], gathered.at[me], own_sem)
    fetch = pltpu.make_async_copy(
        spectra_ref.at[:, pl.ds(0, held_rows), :, pl.ds(part * width, width)], raw, raw_sem
    )
    sites = pltpu.make_async_copy(saved_ref, site, site_sem)
    fetch.start()

    @pl.when(inner)
    def _():
        own.start()

    barrier = pltpu.get_barrier_semaphore()
    everyone = 2 * size_px

    @pl.loop(1, everyone)
    def _(turn):
        peer = lax.rem(turn_of * size_px + me + turn, everyone)
        pl.semaphore_signal(
            barrier,
            inc=1,
            device_id={"chain": lax.div(peer, size_px), "px": lax.rem(peer, size_px)},
            device_id_type=pl.DeviceIdType.MESH,
        )

    pl.semaphore_wait(barrier, everyone - 1)

    def send_own(chunk):
        own_on(chunk).start()
        to_mate(chunk).start()

    def convert():
        fetch.wait()
        block = 16
        for slot in range(slots):

            @pl.loop(0, middle // block)
            def _(at):
                span = pl.ds(pl.multiple_of(at * block, block), block)
                piece = raw[slot, span].astype(jnp.float32)
                kernels[count + 1 :, slot, span, :] = jnp.swapaxes(piece, 0, 1)

            piece = raw[slot, middle : middle + block].astype(jnp.float32)
            kernels[count + 1 :, slot, middle : middle + 8, :] = jnp.swapaxes(piece[:8], 0, 1)

    span = planes // chunks

    def weights_out(chunk):
        return pltpu.make_async_copy(
            weighed.at[lax.rem(chunk, 2)],
            weight_ref.at[:, pl.ds(chunk * span, span)],
            weigh_sem.at[chunk],
        )

    def weigh(chunk):
        @pl.when(chunk >= 2)
        def _():
            weights_out(chunk - 2).wait()

        for slot in range(slots):
            index = chosen_ref[slot].astype(jnp.float32)
            turns = site[pl.ds(chunk * span, span)] * (index * (1.0 / 16.0))
            value = cosine_turns(turns) * (index * (math.pi / 8.0 * scale))
            weighed[lax.rem(chunk, 2), slot] = value
        weights_out(chunk).start()

    def relay(chunk):
        pass_on(1, mate, chunk).wait_recv()
        pass_on(1, mate, chunk).start()

        @pl.when(inner)
        def _():
            for kind, owner in ((2, behind), (3, behind_mate)):
                pass_on(kind, owner, chunk).wait_recv()
                pass_on(kind, owner, chunk).start()

        @pl.when(chunk + lead < chunks)
        def _():
            send_own(chunk + lead)

    def relay_kernels(chunk):
        @pl.loop(0, step)
        def _(at):
            pass_kernel(chunk * step + at)

        with_last(chunk, pass_kernel)

    def compute(chunk):
        for owner in (onward, onward + 1 - 2 * column):
            pass_on(1, owner, chunk).wait_recv()
        further = jnp.where(lower, onward + 2, onward - 2)
        for owner in (further, further + 1 - 2 * column):
            pass_on(1, owner, chunk).wait_recv()

        @pl.loop(0, step)
        def _(at):
            await_kernel(chunk * step + at)

        with_last(chunk, await_kernel)
        own_sites = pl.ds(pl.multiple_of(base * planes, half * planes), half * planes)
        top = lax.broadcasted_iota(jnp.int32, (middle, 2 * width), 0) == 0

        @pl.loop(0, step)
        def _(at):
            line = chunk * step + at
            first, second = 2 * line, 2 * line + 1
            columns = jnp.concatenate(
                [gathered[:, row].reshape(one, width) for row in (first, second)], axis=1
            )
            spectrum = from_left(ahead_ref[...], columns)
            plain = held_at(line)
            leading = (line == leading_place) & (column == 0)
            mirrored = jnp.where(leading, held_at(jnp.int32(count)), plain)
            for slot in range(slots):
                body = jnp.concatenate(
                    [kernels[plain, slot, 0:middle], kernels[mirrored, slot, 0:middle]], axis=1
                )
                edge = jnp.concatenate(
                    [
                        kernels[plain, slot, middle : middle + 1],
                        kernels[mirrored, slot, middle : middle + 1],
                    ],
                    axis=1,
                )
                factor = jnp.concatenate([body, jnp.where(top, edge, body)], axis=0)
                result = from_left(behind_ref[own_sites, :], spectrum * factor)
                product[slot, :, first] = result[:, :width].reshape(half, planes, width)
                product[slot, :, second] = result[:, width:].reshape(half, planes, width)

        for slot in range(slots):

            @pl.loop(0, half)
            def _(turn):
                receiver = base + turn

                @pl.when(receiver != me)
                def _():
                    back(slot, chunk, receiver).start()

            home(slot, chunk).start()

    def send_kernels(begin, length):
        @pl.loop(0, length)
        def _(at):
            @pl.when(begin + at < local)
            def _():
                each_kernel_row(begin + at, lambda copy: copy.start())

    pl.loop(0, lead)(send_own)

    @pl.when(inner)
    def _():
        convert()
        extra_copy(lambda copy: copy.start())

        send_kernels(jnp.int32(0), first_rows)
        own.wait()
        sites.start()

        @pl.loop(0, depth)
        def _(chunk):
            relay(chunk)
            relay_kernels(chunk)

        sites.wait()

        @pl.loop(0, chunks)
        def _(chunk):
            send_kernels(first_rows + chunk * per_chunk, per_chunk)

            @pl.when(chunk + depth < chunks)
            def _():
                relay(chunk + depth)
                relay_kernels(chunk + depth)

            weigh(chunk)
            compute(chunk)

    @pl.when(outer)
    def _():
        pl.loop(0, early)(relay)
        sites.start()
        convert()
        extra_copy(lambda copy: copy.start())

        @pl.loop(early, chunks)
        def _(chunk):
            relay(chunk)
            send_kernels((chunk - early) * pace, pace)

        sites.wait()
        pl.loop(0, chunks)(weigh)

    @pl.loop(0, chunks)
    def _(chunk):
        to_mate(chunk).wait_send()
        own_on(chunk).wait_send()
        pass_on(1, mate, chunk).wait_send()
        for slot in range(slots):
            back_arrival(slot, chunk, 1 - column).wait_recv()

        @pl.when(outer)
        def _():
            for slot in range(slots):
                back_arrival(slot, chunk, column).wait_recv()

        @pl.when(inner)
        def _():
            for kind, owner in ((2, behind), (3, behind_mate)):
                pass_on(kind, owner, chunk).wait_send()
            for slot in range(slots):
                home(slot, chunk).wait()

                @pl.loop(0, half)
                def _(turn):
                    receiver = base + turn

                    @pl.when(receiver != me)
                    def _():
                        back(slot, chunk, receiver).wait_send()

    @pl.loop(chunks - 2, chunks)
    def _(chunk):
        weights_out(chunk).wait()

    @pl.loop(0, local)
    def _(turn):
        each_kernel_row(turn, lambda copy: copy.wait_send())

    extra_copy(lambda copy: copy.wait_send())

    @pl.when(inner)
    def _():
        def passed(place):
            @pl.when(arrives(place) & firsthand(place))
            def _():
                kernel_on(place).wait_send()

        pl.loop(0, count)(passed)

        @pl.when(column == 0)
        def _():
            passed(jnp.int32(count))


def second_order(length, blocks):
    count, local = length // 4, length // (2 * blocks)
    quarter = local // 2
    side, place = np.divmod(np.arange(2 * count), count)
    group, at = np.divmod(place, count // 2)
    block = 2 - 2 * group + at % 2
    value = local * block + quarter - 1 - at // 2 + quarter * side
    mirror = np.where(value == 0, length // 2, length - value)
    return np.stack([value, mirror], axis=1).reshape(-1)


def first_order(length):
    counter = np.arange(length // 2)
    return np.concatenate([counter, np.where(counter == 0, length // 2, length - counter)])


def kernel_path(adjoint, saved, spectra, chosen):
    size_px, size_py = lax.axis_size("px"), lax.axis_size("py")
    planes, lines, three = adjoint.shape
    one, two = planes * size_px, lines * size_py
    width, local, slots = three // size_py, spectra.shape[2], chosen.shape[0]
    whole = lambda table: pl.BlockSpec(table.shape, lambda *at: (0,) * table.ndim)
    anywhere = pl.BlockSpec(memory_space=pl.ANY)
    f32 = jnp.float32
    block = 8
    steps = planes // block
    dma = pltpu.SemaphoreType.DMA
    right_three = as_three(hartley(three), 0)
    half = size_px // 2
    order = second_order(two, half)
    order_one = first_order(one)
    left_two = as_three(hartley(two)[order], 1)
    left_two_back = as_three(hartley(two)[:, order], 1)
    scale = 1.0 / (one * two * three)
    left_one = as_three(hartley(one)[order_one], 1)
    left_one_back = as_three(hartley(one)[:, order_one], 1)

    field = pl.pallas_call(
        functools.partial(third_kernel, steps),
        grid=(steps,),
        in_specs=[pl.BlockSpec((block, lines, three), lambda i: (i, 0, 0)), whole(right_three)],
        out_specs=anywhere,
        out_shape=jax.ShapeDtypeStruct((size_py, planes, lines, width), f32),
        scratch_shapes=[pltpu.VMEM((size_py, planes, lines, width), f32)] + [dma((steps,))] * 3,
        compiler_params=params(collective_id=1, has_side_effects=True),
        name="third",
    )(adjoint, right_three)
    field = pl.pallas_call(
        second_kernel,
        grid=(planes // block,),
        in_specs=[
            pl.BlockSpec((size_py, block, lines, width), lambda i: (0, i, 0, 0)),
            whole(left_two),
        ],
        out_specs=pl.BlockSpec((2, two // 2, block, width), lambda i: (0, 0, i, 0)),
        out_shape=jax.ShapeDtypeStruct((2, two // 2, planes, width), f32),
        scratch_shapes=[pltpu.VMEM((block, two, width), f32)],
        compiler_params=params(),
        name="second",
    )(field, left_two)
    count = two // 4
    chunks = math.gcd(count, planes)
    in_vmem = pl.BlockSpec(memory_space=pltpu.VMEM)
    field, weights = pl.pallas_call(
        functools.partial(middle_kernel, chunks, scale),
        in_specs=[pl.BlockSpec(memory_space=pltpu.SMEM)] + [anywhere] * 3 + [in_vmem] * 2,
        out_specs=[anywhere, anywhere],
        out_shape=[
            jax.ShapeDtypeStruct((slots, 2, two // 2, planes, width), f32),
            jax.ShapeDtypeStruct((slots, planes, lines, three), f32),
        ],
        scratch_shapes=[
            pltpu.VMEM((planes, lines, three), f32),
            pltpu.VMEM((2, slots, planes // chunks, lines, three), f32),
            pltpu.VMEM((size_px, two // 2, planes, width), f32),
            pltpu.VMEM((slots, one // 2 + 16, local, width), spectra.dtype),
            pltpu.VMEM((count + 1 + local, slots, one // 2 + 8, width), f32),
            pltpu.VMEM((slots, half, two // 2, planes, width), f32),
            dma((chunks,)),
            dma((4, chunks)),
            dma((size_px, chunks)),
            dma((local,)),
            dma((count + 1,)),
            dma((count + 1,)),
            dma,
            dma((slots, chunks, half)),
            dma((slots, chunks, 2)),
            dma((slots, chunks)),
            dma,
            dma,
            dma,
            dma((chunks,)),
        ],
        compiler_params=params(collective_id=0, has_side_effects=True),
        name="middle",
    )(chosen, field, spectra, saved, left_one, left_one_back)
    field = pl.pallas_call(
        functools.partial(second_back_kernel, slots * steps),
        grid=(slots, steps),
        in_specs=[
            pl.BlockSpec((1, 2, two // 2, block, width), lambda j, i: (j, 0, 0, i, 0)),
            whole(left_two_back),
        ],
        out_specs=anywhere,
        out_shape=jax.ShapeDtypeStruct((size_py, slots, planes, lines, width), f32),
        scratch_shapes=[
            pltpu.VMEM((block, two, width), f32),
            pltpu.VMEM((size_py, slots, planes, lines, width), f32),
        ]
        + [dma((slots * steps,))] * 3,
        compiler_params=params(collective_id=2, has_side_effects=True),
        name="second_back",
    )(field, left_two_back)
    piece = 8
    return pl.pallas_call(
        third_back_kernel,
        grid=(planes // piece,),
        in_specs=[
            pl.BlockSpec((size_py, slots, piece, lines, width), lambda i: (0, 0, i, 0, 0)),
            pl.BlockSpec((slots, piece, lines, three), lambda i: (0, i, 0, 0)),
            whole(right_three),
        ],
        out_specs=pl.BlockSpec((piece, lines, three), lambda i: (i, 0, 0)),
        out_shape=jax.ShapeDtypeStruct((planes, lines, three), f32),
        compiler_params=params(),
        name="third_back",
    )(field, weights, right_three)


def on_device(adjoint, saved, spectra, freq_index, picked):
    chosen = chosen_index(freq_index, picked)
    width = adjoint.shape[2] // lax.axis_size("py")
    even = lax.axis_size("px") == 8 and lax.axis_size("py") == 2 and lax.axis_size("chain") == 2
    if even and adjoint.shape[0] % 8 == 0 and spectra.shape[2] % 32 == 0 and width % 128 == 0:
        return kernel_path(adjoint, saved, spectra, chosen)
    return plain_path(adjoint, saved, spectra, chosen)


def solution(mesh):
    placed = (
        P(("chain", "px"), "py", None),
        P(("chain", "px"), "py", None),
        P(None, None, "px", None),
        P(),
        P(),
    )
    return jax.shard_map(
        on_device,
        mesh=mesh,
        in_specs=placed,
        out_specs=P(("chain", "px"), "py", None),
        check_vma=False,
    )
```

```python
import functools
import math

import jax
import jax.numpy as jnp
import numpy as np
from jax import lax
from jax.experimental import pallas as pl
from jax.experimental.pallas import tpu as pltpu
from jax.sharding import PartitionSpec as P


def hartley(length):
    counter = np.arange(length, dtype=np.int64)
    angle = (counter[:, None] * counter[None, :] % length) * (2.0 * np.pi / length)
    return np.cos(angle) + np.sin(angle)


def chosen_index(freq_index, picked):
    ids = jnp.arange(freq_index.shape[0], dtype=jnp.int32)
    return jnp.sum(jnp.where(ids[None, :] == picked[:, None], freq_index[None, :], 0), axis=1)


def along(equation, field, table):
    return jnp.einsum(equation, field, jnp.asarray(table, jnp.float32), precision=lax.Precision.HIGH)


def plain_path(adjoint, saved, spectra, chosen):
    size_px, size_py = lax.axis_size("px"), lax.axis_size("py")
    one, two, three = adjoint.shape[0] * size_px, adjoint.shape[1] * size_py, adjoint.shape[2]
    t_one, t_two, t_three = hartley(one), hartley(two), hartley(three)
    width = three // size_py
    field = along("abc,cz->abz", adjoint, t_three)
    field = lax.all_to_all(field, "py", split_axis=2, concat_axis=1, tiled=True)
    field = along("abc,bz->azc", field, t_two)
    field = lax.all_to_all(field, "px", split_axis=1, concat_axis=0, tiled=True)
    spectrum = along("abc,az->zbc", field, t_one)
    kernels = lax.dynamic_slice_in_dim(spectra, lax.axis_index("py") * width, width, 3)
    omegas = chosen.astype(jnp.float32) * (math.pi / 8.0)
    scale = 1.0 / (one * two * three)
    total = jnp.zeros(saved.shape, jnp.float32)
    for slot in range(chosen.shape[0]):
        back = along("abc,az->zbc", spectrum * kernels[slot].astype(jnp.float32), t_one)
        back = lax.all_to_all(back, "px", split_axis=0, concat_axis=1, tiled=True)
        back = along("abc,bz->azc", back, t_two)
        back = lax.all_to_all(back, "py", split_axis=1, concat_axis=2, tiled=True)
        back = along("abc,cz->abz", back, t_three) * scale
        total = total + omegas[slot] * jnp.cos(omegas[slot] * saved) * back
    return total


def as_three(matrix, axis):
    high = matrix.astype(jnp.bfloat16)
    low = (matrix - high.astype(np.float64)).astype(jnp.bfloat16)
    order = (high, high, low)
    return jnp.asarray(np.concatenate(order, axis=axis))


def split(value, axis):
    high = value.astype(jnp.bfloat16)
    low = (value - high.astype(jnp.float32)).astype(jnp.bfloat16)
    return jnp.concatenate([high, low, high], axis=axis)


def from_right(rows, table):
    return jnp.dot(split(rows, 1), table, preferred_element_type=jnp.float32)


def from_left(table, columns):
    return jnp.dot(table, split(columns, 0), preferred_element_type=jnp.float32)


def params(**more):
    return pltpu.CompilerParams(vmem_limit_bytes=58 << 20, **more)


def core_exchange(step, steps, source, target, sems):
    send_sem, recv_sem, own_sem = sems
    me = lax.axis_index("py")
    other = 1 - me

    def away(at, sender, receiver):
        return pltpu.make_async_remote_copy(
            src_ref=source(receiver, at),
            dst_ref=target(sender, at),
            send_sem=send_sem.at[at],
            recv_sem=recv_sem.at[at],
            device_id={"py": receiver},
            device_id_type=pl.DeviceIdType.MESH,
        )

    def stay(at):
        return pltpu.make_async_copy(source(me, at), target(me, at), own_sem.at[at])

    away(step, me, other).start()
    stay(step).start()

    @pl.when(step == steps - 1)
    def _():
        @pl.loop(0, steps)
        def _(at):
            away(at, me, other).wait_send()
            away(at, other, me).wait_recv()
            stay(at).wait()


def greet_core():
    barrier = pltpu.get_barrier_semaphore()
    other = 1 - lax.axis_index("py")
    pl.semaphore_signal(
        barrier, inc=1, device_id={"py": other}, device_id_type=pl.DeviceIdType.MESH
    )
    pl.semaphore_wait(barrier, 1)


def third_kernel(steps, field_ref, table_ref, out_ref, mine, *sems):
    planes, lines, three = field_ref.shape
    parts, width = mine.shape[0], mine.shape[3]
    step = pl.program_id(0)
    pl.when(step == 0)(greet_core)

    def rows(at):
        return pl.ds(pl.multiple_of(at * planes, planes), planes)

    result = from_right(field_ref[...].reshape(planes * lines, three), table_ref[...])
    for part in range(parts):
        piece = result[:, part * width : (part + 1) * width]
        mine[part, rows(step)] = piece.reshape(planes, lines, width)
    core_exchange(
        step,
        steps,
        lambda part, at: mine.at[part, rows(at)],
        lambda part, at: out_ref.at[part, rows(at)],
        sems,
    )


def second_kernel(field_ref, table_ref, out_ref, held):
    parts, planes, _, width = field_ref.shape
    size_px, local, _, _ = out_ref.shape
    for plane in range(0, planes, 2):
        sides = [
            jnp.concatenate([field_ref[part, at] for part in range(parts)], axis=0)
            for at in (plane, plane + 1)
        ]
        result = from_left(table_ref[...], jnp.concatenate(sides, axis=1))
        held[plane] = result[:, :width]
        held[plane + 1] = result[:, width:]
    for peer in range(size_px):
        out_ref[peer] = jnp.swapaxes(held[:, peer * local : (peer + 1) * local, :], 0, 1)


def cosine_turns(turns):
    turns = turns - jnp.floor(turns + 0.5)
    square = turns * turns * (4.0 * math.pi * math.pi)
    value = jnp.full_like(square, 1.0 / math.factorial(20))
    for order in range(9, -1, -1):
        value = value * square + (-1.0) ** order / math.factorial(2 * order)
    return value


def second_back_kernel(steps, field_ref, table_ref, out_ref, held, mine, *sems):
    _, groups, local, planes, width = field_ref.shape
    parts, lines = mine.shape[0], mine.shape[3]
    inner = steps // mine.shape[1]
    step = pl.program_id(0) * inner + pl.program_id(1)
    slot = pl.program_id(0)
    begin = pl.program_id(1) * planes
    pl.when(step == 0)(greet_core)
    for group in range(groups):
        held[:, group * local : (group + 1) * local, :] = jnp.swapaxes(field_ref[0, group], 0, 1)
    for plane in range(0, planes, 2):
        columns = jnp.concatenate([held[plane], held[plane + 1]], axis=1)
        result = from_left(table_ref[...], columns)
        for part in range(parts):
            rows = result[part * lines : (part + 1) * lines]
            mine[part, slot, begin + plane] = rows[:, :width]
            mine[part, slot, begin + plane + 1] = rows[:, width:]

    def block(ref):
        return lambda part, at: ref.at[part, at // inner, pl.ds((at % inner) * planes, planes)]

    core_exchange(step, steps, block(mine), block(out_ref), sems)


def third_back_kernel(field_ref, weight_ref, table_ref, out_ref):
    parts, slots, planes, lines, width = field_ref.shape
    three = parts * width
    total = None
    for slot in range(slots):
        sides = [field_ref[part, slot].reshape(planes * lines, width) for part in range(parts)]
        field = from_right(jnp.concatenate(sides, axis=1), table_ref[...])
        term = weight_ref[slot].reshape(planes * lines, three) * field
        total = term if total is None else total + term
    out_ref[...] = total.reshape(planes, lines, three)


def middle_kernel(
    chunks,
    scale,
    chosen_ref,
    field_ref,
    spectra_ref,
    saved_ref,
    ahead_ref,
    behind_ref,
    out_ref,
    weight_ref,
    site,
    weighed,
    gathered,
    raw,
    kernels,
    product,
    mate_send,
    next_send,
    go_recv,
    kernel_send,
    kernel_recv,
    kernel_pass,
    extra_send,
    back_send,
    back_recv,
    home_sem,
    own_sem,
    raw_sem,
    site_sem,
    weigh_sem,
):
    _, rows_all, planes, width = field_ref.shape
    size_px, slots = gathered.shape[0], raw.shape[0]
    half, count = size_px // 2, rows_all // 2
    held_rows, local = raw.shape[1], raw.shape[2]
    one, middle, quarter = size_px * planes, size_px * planes // 2, local // 2
    two = size_px * local
    step = count // chunks
    lead, depth, early = 2, 1, min(10, chunks // 2)
    per_chunk = -(-2 * local // chunks)
    first_rows = min(local, 4 * per_chunk)
    pace = -(-local // (chunks - early)) + 0
    me = lax.axis_index("px")
    part = lax.axis_index("py")
    turn_of = lax.axis_index("chain")
    lower = me < half
    base = jnp.where(lower, 0, half)
    column = lax.rem(me, 2)
    mate = me + 1 - 2 * column
    onward = jnp.where(lower, me + 2, me - 2)
    behind = jnp.where(lower, me - 2, me + 2)
    behind_mate = behind + 1 - 2 * column
    inner = (me >= half - 2) & (me < half + 2)
    outer = jnp.logical_not(inner)
    centre = jnp.where(lower, half - 2, half)

    def to(index):
        return dict(device_id={"px": index}, device_id_type=pl.DeviceIdType.MESH)

    def across():
        return dict(device_id={"chain": 1 - turn_of}, device_id_type=pl.DeviceIdType.MESH)

    def rows(chunk):
        return pl.ds(pl.multiple_of(chunk * 2 * step, 2 * step), 2 * step)

    def to_mate(chunk):
        return pltpu.make_async_remote_copy(
            src_ref=field_ref.at[1 - column, rows(chunk)],
            dst_ref=gathered.at[me, rows(chunk)],
            send_sem=mate_send.at[chunk],
            recv_sem=go_recv.at[me, chunk],
            **to(mate),
        )

    def own_on(chunk):
        return pltpu.make_async_remote_copy(
            src_ref=field_ref.at[column, rows(chunk)],
            dst_ref=gathered.at[me, rows(chunk)],
            send_sem=next_send.at[0, chunk],
            recv_sem=go_recv.at[me, chunk],
            **to(onward),
        )

    def pass_on(kind, owner, chunk):
        return pltpu.make_async_remote_copy(
            src_ref=gathered.at[owner, rows(chunk)],
            dst_ref=gathered.at[owner, rows(chunk)],
            send_sem=next_send.at[kind, chunk],
            recv_sem=go_recv.at[owner, chunk],
            **to(onward),
        )

    def back(slot, chunk, receiver):
        return pltpu.make_async_remote_copy(
            src_ref=product.at[slot, receiver - base, rows(chunk)],
            dst_ref=out_ref.at[slot, column, rows(chunk)],
            send_sem=back_send.at[slot, chunk, receiver - base],
            recv_sem=back_recv.at[slot, chunk, column],
            **to(receiver),
        )

    def back_arrival(slot, chunk, side):
        return pltpu.make_async_remote_copy(
            src_ref=product.at[slot, 0, rows(chunk)],
            dst_ref=out_ref.at[slot, side, rows(chunk)],
            send_sem=back_send.at[slot, chunk, 0],
            recv_sem=back_recv.at[slot, chunk, side],
            **to(mate),
        )

    def home(slot, chunk):
        return pltpu.make_async_copy(
            product.at[slot, me - base, rows(chunk)],
            out_ref.at[slot, column, rows(chunk)],
            home_sem.at[slot, chunk],
        )

    def frequency(place):
        group, at = lax.div(place, count // 2), lax.rem(place, count // 2)
        block = 2 - 2 * group + lax.rem(at, 2)
        return local * block + quarter - 1 - lax.div(at, 2) + quarter * column

    def source(place):
        value = jnp.where(place == count, two // 2, frequency(place))
        above = jnp.where(value == 0, 0, lax.div(two - value, local))
        holder = jnp.where(lower, lax.div(value, local), above)
        row = jnp.where(lower | (value == 0), lax.rem(value, local), lax.rem(two - value, local))
        return jnp.where(place == count, half, holder), row

    def held_at(place):
        holder, row = source(place)
        return jnp.where(holder == me, count + 1 + row, place)

    def firsthand(place):
        return lax.rem(lax.div(place, 2), 2) == turn_of

    def kernel_row(turn):
        turn = jnp.where(lower, turn, lax.rem(turn + local - 2, local))
        offset = quarter - 1 - lax.div(turn, 2) + quarter * lax.rem(turn, 2)
        row = jnp.where(lower, offset, lax.rem(local - offset, local))
        value = jnp.where(lower, local * me + row, two - local * me - row)
        block, inside = lax.div(value, local), lax.rem(value, local)
        side, level = lax.div(inside, quarter), lax.rem(inside, quarter)
        place = jnp.where(block >= 2, 0, count // 2) + 2 * (quarter - 1 - level) + lax.rem(block, 2)
        return row, side, jnp.where(value == two // 2, count, place)

    def kernel_copy(row, place, receiver, sem):
        return pltpu.make_async_remote_copy(
            src_ref=kernels.at[count + 1 + row],
            dst_ref=kernels.at[place],
            send_sem=sem,
            recv_sem=kernel_recv.at[place],
            **to(receiver),
        )

    def each_kernel_row(turn, act):
        row, side, place = kernel_row(turn)

        @pl.when((centre + side != me) & firsthand(place))
        def _():
            act(kernel_copy(row, place, centre + side, kernel_send.at[row]))

    def extra_copy(act):
        for sender, place, receiver in ((0, count - 2, half), (half, count, half - 2)):

            @pl.when((me == sender) & firsthand(jnp.int32(place)))
            def _():
                act(kernel_copy(0, place, jnp.int32(receiver), extra_send))

    def kernel_arrival(place):
        return kernel_copy(0, place, mate, extra_send)

    def kernel_on(place):
        return pltpu.make_async_remote_copy(
            src_ref=kernels.at[place],
            dst_ref=kernels.at[place],
            send_sem=kernel_pass.at[place],
            recv_sem=kernel_recv.at[place],
            **across(),
        )

    def arrives(place):
        return source(place)[0] != me

    leading_place = count - 2

    def pass_kernel(place):
        @pl.when(arrives(place) & firsthand(place))
        def _():
            kernel_arrival(place).wait_recv()
            kernel_on(place).start()

    def await_kernel(place):
        @pl.when(arrives(place) & jnp.logical_not(firsthand(place)))
        def _():
            kernel_arrival(place).wait_recv()

    def with_last(chunk, act):
        @pl.when((chunk == leading_place // step) & (column == 0))
        def _():
            act(jnp.int32(count))

    own = pltpu.make_async_copy(field_ref.at[column], gathered.at[me], own_sem)
    fetch = pltpu.make_async_copy(
        spectra_ref.at[:, pl.ds(0, held_rows), :, pl.ds(part * width, width)], raw, raw_sem
    )
    sites = pltpu.make_async_copy(saved_ref, site, site_sem)
    fetch.start()

    @pl.when(inner)
    def _():
        own.start()

    barrier = pltpu.get_barrier_semaphore()
    everyone = 2 * size_px

    @pl.loop(1, everyone)
    def _(turn):
        peer = lax.rem(turn_of * size_px + me + turn, everyone)
        pl.semaphore_signal(
            barrier,
            inc=1,
            device_id={"chain": lax.div(peer, size_px), "px": lax.rem(peer, size_px)},
            device_id_type=pl.DeviceIdType.MESH,
        )

    pl.semaphore_wait(barrier, everyone - 1)

    def send_own(chunk):
        to_mate(chunk).start()
        own_on(chunk).start()

    def convert():
        fetch.wait()
        block = 16
        for slot in range(slots):

            @pl.loop(0, middle // block)
            def _(at):
                span = pl.ds(pl.multiple_of(at * block, block), block)
                piece = raw[slot, span].astype(jnp.float32)
                kernels[count + 1 :, slot, span, :] = jnp.swapaxes(piece, 0, 1)

            piece = raw[slot, middle : middle + block].astype(jnp.float32)
            kernels[count + 1 :, slot, middle : middle + 8, :] = jnp.swapaxes(piece[:8], 0, 1)

    span = planes // chunks

    def weights_out(chunk):
        return pltpu.make_async_copy(
            weighed.at[lax.rem(chunk, 2)],
            weight_ref.at[:, pl.ds(chunk * span, span)],
            weigh_sem.at[chunk],
        )

    def weigh(chunk):
        @pl.when(chunk >= 2)
        def _():
            weights_out(chunk - 2).wait()

        for slot in range(slots):
            index = chosen_ref[slot].astype(jnp.float32)
            turns = site[pl.ds(chunk * span, span)] * (index * (1.0 / 16.0))
            value = cosine_turns(turns) * (index * (math.pi / 8.0 * scale))
            weighed[lax.rem(chunk, 2), slot] = value
        weights_out(chunk).start()

    def relay(chunk):
        pass_on(1, mate, chunk).wait_recv()
        pass_on(1, mate, chunk).start()

        @pl.when(inner)
        def _():
            for kind, owner in ((2, behind), (3, behind_mate)):
                pass_on(kind, owner, chunk).wait_recv()
                pass_on(kind, owner, chunk).start()

        @pl.when(chunk + lead < chunks)
        def _():
            send_own(chunk + lead)

    def relay_kernels(chunk):
        @pl.loop(0, step)
        def _(at):
            pass_kernel(chunk * step + at)

        with_last(chunk, pass_kernel)

    def compute(chunk):
        for owner in (onward, onward + 1 - 2 * column):
            pass_on(1, owner, chunk).wait_recv()
        further = jnp.where(lower, onward + 2, onward - 2)
        for owner in (further, further + 1 - 2 * column):
            pass_on(1, owner, chunk).wait_recv()

        @pl.loop(0, step)
        def _(at):
            await_kernel(chunk * step + at)

        with_last(chunk, await_kernel)
        own_sites = pl.ds(pl.multiple_of(base * planes, half * planes), half * planes)
        top = lax.broadcasted_iota(jnp.int32, (middle, 2 * width), 0) == 0

        @pl.loop(0, step)
        def _(at):
            line = chunk * step + at
            first, second = 2 * line, 2 * line + 1
            columns = jnp.concatenate(
                [gathered[:, row].reshape(one, width) for row in (first, second)], axis=1
            )
            spectrum = from_left(ahead_ref[...], columns)
            plain = held_at(line)
            leading = (line == leading_place) & (column == 0)
            mirrored = jnp.where(leading, held_at(jnp.int32(count)), plain)
            for slot in range(slots):
                body = jnp.concatenate(
                    [kernels[plain, slot, 0:middle], kernels[mirrored, slot, 0:middle]], axis=1
                )
                edge = jnp.concatenate(
                    [
                        kernels[plain, slot, middle : middle + 1],
                        kernels[mirrored, slot, middle : middle + 1],
                    ],
                    axis=1,
                )
                factor = jnp.concatenate([body, jnp.where(top, edge, body)], axis=0)
                result = from_left(behind_ref[own_sites, :], spectrum * factor)
                product[slot, :, first] = result[:, :width].reshape(half, planes, width)
                product[slot, :, second] = result[:, width:].reshape(half, planes, width)

        for slot in range(slots):

            @pl.loop(0, half)
            def _(turn):
                receiver = base + turn

                @pl.when(receiver != me)
                def _():
                    back(slot, chunk, receiver).start()

            home(slot, chunk).start()

    def send_kernels(begin, length):
        @pl.loop(0, length)
        def _(at):
            @pl.when(begin + at < local)
            def _():
                each_kernel_row(begin + at, lambda copy: copy.start())

    pl.loop(0, lead)(send_own)

    @pl.when(inner)
    def _():
        convert()
        extra_copy(lambda copy: copy.start())

        send_kernels(jnp.int32(0), first_rows)
        own.wait()
        sites.start()

        @pl.loop(0, depth)
        def _(chunk):
            relay(chunk)
            relay_kernels(chunk)

        sites.wait()

        @pl.loop(0, chunks)
        def _(chunk):
            send_kernels(first_rows + chunk * per_chunk, per_chunk)

            @pl.when(chunk + depth < chunks)
            def _():
                relay(chunk + depth)
                relay_kernels(chunk + depth)

            weigh(chunk)
            compute(chunk)

    @pl.when(outer)
    def _():
        pl.loop(0, early)(relay)
        sites.start()
        convert()
        extra_copy(lambda copy: copy.start())

        @pl.loop(early, chunks)
        def _(chunk):
            relay(chunk)
            send_kernels((chunk - early) * pace, pace)

        sites.wait()
        pl.loop(0, chunks)(weigh)

    @pl.loop(0, chunks)
    def _(chunk):
        to_mate(chunk).wait_send()
        own_on(chunk).wait_send()
        pass_on(1, mate, chunk).wait_send()
        for slot in range(slots):
            back_arrival(slot, chunk, 1 - column).wait_recv()

        @pl.when(outer)
        def _():
            for slot in range(slots):
                back_arrival(slot, chunk, column).wait_recv()

        @pl.when(inner)
        def _():
            for kind, owner in ((2, behind), (3, behind_mate)):
                pass_on(kind, owner, chunk).wait_send()
            for slot in range(slots):
                home(slot, chunk).wait()

                @pl.loop(0, half)
                def _(turn):
                    receiver = base + turn

                    @pl.when(receiver != me)
                    def _():
                        back(slot, chunk, receiver).wait_send()

    @pl.loop(chunks - 2, chunks)
    def _(chunk):
        weights_out(chunk).wait()

    @pl.loop(0, local)
    def _(turn):
        each_kernel_row(turn, lambda copy: copy.wait_send())

    extra_copy(lambda copy: copy.wait_send())

    @pl.when(inner)
    def _():
        def passed(place):
            @pl.when(arrives(place) & firsthand(place))
            def _():
                kernel_on(place).wait_send()

        pl.loop(0, count)(passed)

        @pl.when(column == 0)
        def _():
            passed(jnp.int32(count))


def second_order(length, blocks):
    count, local = length // 4, length // (2 * blocks)
    quarter = local // 2
    side, place = np.divmod(np.arange(2 * count), count)
    group, at = np.divmod(place, count // 2)
    block = 2 - 2 * group + at % 2
    value = local * block + quarter - 1 - at // 2 + quarter * side
    mirror = np.where(value == 0, length // 2, length - value)
    return np.stack([value, mirror], axis=1).reshape(-1)


def first_order(length):
    counter = np.arange(length // 2)
    return np.concatenate([counter, np.where(counter == 0, length // 2, length - counter)])


def kernel_path(adjoint, saved, spectra, chosen):
    size_px, size_py = lax.axis_size("px"), lax.axis_size("py")
    planes, lines, three = adjoint.shape
    one, two = planes * size_px, lines * size_py
    width, local, slots = three // size_py, spectra.shape[2], chosen.shape[0]
    whole = lambda table: pl.BlockSpec(table.shape, lambda *at: (0,) * table.ndim)
    anywhere = pl.BlockSpec(memory_space=pl.ANY)
    f32 = jnp.float32
    block = 8
    steps = planes // block
    dma = pltpu.SemaphoreType.DMA
    right_three = as_three(hartley(three), 0)
    half = size_px // 2
    order = second_order(two, half)
    order_one = first_order(one)
    left_two = as_three(hartley(two)[order], 1)
    left_two_back = as_three(hartley(two)[:, order], 1)
    scale = 1.0 / (one * two * three)
    left_one = as_three(hartley(one)[order_one], 1)
    left_one_back = as_three(hartley(one)[:, order_one], 1)

    field = pl.pallas_call(
        functools.partial(third_kernel, steps),
        grid=(steps,),
        in_specs=[pl.BlockSpec((block, lines, three), lambda i: (i, 0, 0)), whole(right_three)],
        out_specs=anywhere,
        out_shape=jax.ShapeDtypeStruct((size_py, planes, lines, width), f32),
        scratch_shapes=[pltpu.VMEM((size_py, planes, lines, width), f32)] + [dma((steps,))] * 3,
        compiler_params=params(collective_id=1, has_side_effects=True),
        name="third",
    )(adjoint, right_three)
    field = pl.pallas_call(
        second_kernel,
        grid=(planes // block,),
        in_specs=[
            pl.BlockSpec((size_py, block, lines, width), lambda i: (0, i, 0, 0)),
            whole(left_two),
        ],
        out_specs=pl.BlockSpec((2, two // 2, block, width), lambda i: (0, 0, i, 0)),
        out_shape=jax.ShapeDtypeStruct((2, two // 2, planes, width), f32),
        scratch_shapes=[pltpu.VMEM((block, two, width), f32)],
        compiler_params=params(),
        name="second",
    )(field, left_two)
    count = two // 4
    chunks = math.gcd(count, planes)
    in_vmem = pl.BlockSpec(memory_space=pltpu.VMEM)
    field, weights = pl.pallas_call(
        functools.partial(middle_kernel, chunks, scale),
        in_specs=[pl.BlockSpec(memory_space=pltpu.SMEM)] + [anywhere] * 3 + [in_vmem] * 2,
        out_specs=[anywhere, anywhere],
        out_shape=[
            jax.ShapeDtypeStruct((slots, 2, two // 2, planes, width), f32),
            jax.ShapeDtypeStruct((slots, planes, lines, three), f32),
        ],
        scratch_shapes=[
            pltpu.VMEM((planes, lines, three), f32),
            pltpu.VMEM((2, slots, planes // chunks, lines, three), f32),
            pltpu.VMEM((size_px, two // 2, planes, width), f32),
            pltpu.VMEM((slots, one // 2 + 16, local, width), spectra.dtype),
            pltpu.VMEM((count + 1 + local, slots, one // 2 + 8, width), f32),
            pltpu.VMEM((slots, half, two // 2, planes, width), f32),
            dma((chunks,)),
            dma((4, chunks)),
            dma((size_px, chunks)),
            dma((local,)),
            dma((count + 1,)),
            dma((count + 1,)),
            dma,
            dma((slots, chunks, half)),
            dma((slots, chunks, 2)),
            dma((slots, chunks)),
            dma,
            dma,
            dma,
            dma((chunks,)),
        ],
        compiler_params=params(collective_id=0, has_side_effects=True),
        name="middle",
    )(chosen, field, spectra, saved, left_one, left_one_back)
    field = pl.pallas_call(
        functools.partial(second_back_kernel, slots * steps),
        grid=(slots, steps),
        in_specs=[
            pl.BlockSpec((1, 2, two // 2, block, width), lambda j, i: (j, 0, 0, i, 0)),
            whole(left_two_back),
        ],
        out_specs=anywhere,
        out_shape=jax.ShapeDtypeStruct((size_py, slots, planes, lines, width), f32),
        scratch_shapes=[
            pltpu.VMEM((block, two, width), f32),
            pltpu.VMEM((size_py, slots, planes, lines, width), f32),
        ]
        + [dma((slots * steps,))] * 3,
        compiler_params=params(collective_id=2, has_side_effects=True),
        name="second_back",
    )(field, left_two_back)
    piece = 16
    return pl.pallas_call(
        third_back_kernel,
        grid=(planes // piece,),
        in_specs=[
            pl.BlockSpec((size_py, slots, piece, lines, width), lambda i: (0, 0, i, 0, 0)),
            pl.BlockSpec((slots, piece, lines, three), lambda i: (0, i, 0, 0)),
            whole(right_three),
        ],
        out_specs=pl.BlockSpec((piece, lines, three), lambda i: (i, 0, 0)),
        out_shape=jax.ShapeDtypeStruct((planes, lines, three), f32),
        compiler_params=params(),
        name="third_back",
    )(field, weights, right_three)


def on_device(adjoint, saved, spectra, freq_index, picked):
    chosen = chosen_index(freq_index, picked)
    width = adjoint.shape[2] // lax.axis_size("py")
    even = lax.axis_size("px") == 8 and lax.axis_size("py") == 2 and lax.axis_size("chain") == 2
    if even and adjoint.shape[0] % 8 == 0 and spectra.shape[2] % 32 == 0 and width % 128 == 0:
        return kernel_path(adjoint, saved, spectra, chosen)
    return plain_path(adjoint, saved, spectra, chosen)


def solution(mesh):
    placed = (
        P(("chain", "px"), "py", None),
        P(("chain", "px"), "py", None),
        P(None, None, "px", None),
        P(),
        P(),
    )
    return jax.shard_map(
        on_device,
        mesh=mesh,
        in_specs=placed,
        out_specs=P(("chain", "px"), "py", None),
        check_vma=False,
    )
```
